32 devices in a mesh: groups: 2 (over x), dp: 16 (over z, y, core).
Axes of the slice: x: 2, y: 2, z: 4, core: 2. Of those that a mesh axis runs over, the one named last changes fastest.
Arguments:
- clips: bfloat16 [128, 4, 49, 1024], P(('groups', 'dp')), parts along dimension 0, may hold values from -6 to 6
- sign_seeds: int32 [128], P(('groups', 'dp')), parts along dimension 0, may hold values from 0 to 999999
- time_weight: bfloat16 [3, 1024, 1024], replicated, may hold values from -0.109375 to 0.109375
- proj_weight: bfloat16 [1024, 512], replicated, may hold values from -0.1875 to 0.1875
- captions: bfloat16 [640, 512], P(('groups', 'dp')), parts along dimension 0, may hold values from -6 to 6
- caption_rows: int32 [128, 5], P(('groups', 'dp')), parts along dimension 0, may hold values from 0 to 319, as said below
Outputs:
- new_delta: bfloat16 [128, 4, 49, 1024], P(('groups', 'dp')), parts along dimension 0
- clip_loss: float32 [128], P(('groups', 'dp')), parts along dimension 0
The draws below stay inside these ranges and needn't reach their ends.
There are 2 independent parts, one for each index of `groups`. The reference program is written for one: setup_inputs(seed, part) draws one part's arguments, and reference() takes and returns one part's arrays. A program takes and returns all parts, laid end to end along the dimension named above; an argument that names none is the same for every part. Nothing has to cross between parts.
Inputs may be any that keep to these rules, and one draw needn't show every extreme that they name: `caption_rows`: the captions of the clips of one dp device are the 20 caption rows of that device; every caption row belongs to exactly one clip.
All inputs are finite; a program needn't handle non-finite values.
Results may differ from the reference program's by a relative error of at most 0.008.
Values may be sent and summed in bfloat16 or wider, within the bound.
No kernel may reach another device: no remote copies, remote signals or barrier semaphores. Data moves between devices by JAX's collectives and lax.ppermute only.
A program may use at most 64 MiB of HBM per device.

```python
import jax
import jax.numpy as jnp
from jax import lax

C = 1024
E = 512
FRAMES = 4
PIX = 49
CAPS_PER = 5
CLIP_DEV = 4
CLIPS = 64
CAPS = 320


def draw_caption_rows(key, part):
    blocks = CLIPS // CLIP_DEV
    per_block = CAPS_PER * CLIP_DEV
    keys = jax.random.split(key, blocks)
    orders = jax.vmap(lambda single: jax.random.permutation(single, per_block))(keys).astype(jnp.int32)
    offsets = (jnp.arange(blocks, dtype=jnp.int32) * per_block)[:, None]
    return (orders + offsets).reshape(CLIPS, CAPS_PER).astype(jnp.int32)


def set_ends(values, rng, smallest, top_value):
    longest = values.shape.index(max(values.shape))
    spots = []
    for shift in (0, 1):
        where = [jax.random.randint(jax.random.fold_in(rng, axis), (), 0, length) for axis, length in enumerate(values.shape)]
        where[longest] = (where[longest] + shift) % values.shape[longest]
        spots.append(tuple(where))
    return values.at[spots[0]].set(smallest).at[spots[1]].set(top_value)


def block_scale(own_key, shape, shards, smallest, high):
    loudness, own = 1.0, jax.random.fold_in(own_key, 6)
    for dim, blocks in shards:
        heights = jnp.exp(jax.random.uniform(jax.random.fold_in(own, dim), (blocks,), jnp.float32, smallest / len(shards), high / len(shards)))
        loudness = loudness * jnp.repeat(heights, shape[dim] // blocks).reshape([-1 if axis == dim else 1 for axis in range(len(shape))])
    return loudness


def bell_draw(stream_key, dims, scale, bound, cuts=(), held_as=jnp.bfloat16):
    array = scale * jax.random.normal(stream_key, dims, jnp.float32)
    if cuts:
        array = array * block_scale(stream_key, dims, cuts, -0.22, 0.18)
    return jnp.clip(array, -bound, bound).astype(held_as)


def setup_inputs(seed: int = 0, part: int = 0) -> dict:
    splits = jax.random.split(jax.random.key(seed), 7)
    own_keys = jax.random.split(jax.random.fold_in(splits[6], part), 7)
    return {
        "clips": bell_draw(own_keys[0], (CLIPS, FRAMES, PIX, C), 1.0, 6.0, ((0, 16),)),
        "sign_seeds": set_ends(jax.random.randint(own_keys[1], (CLIPS,), 0, 1000000), jax.random.fold_in(own_keys[1], 1), 0, 999999).astype(jnp.int32),
        "time_weight": bell_draw(splits[2], (3, C, C), (3 * C) ** -0.5, 0.109375),
        "proj_weight": bell_draw(splits[3], (C, E), C ** -0.5, 0.1875),
        "captions": bell_draw(own_keys[4], (CAPS, E), 1.0, 6.0, ((0, 16),)),
        "caption_rows": draw_caption_rows(jax.random.fold_in(jax.random.fold_in(splits[6], part), 71), part),
    }


INV_TEMP = 1.0 / 0.07

def sign_field(seeds, frames, pix, chans):
    first = lax.broadcasted_iota(jnp.int32, (frames, pix, chans), 0)
    second = lax.broadcasted_iota(jnp.int32, (frames, pix, chans), 1)
    third = lax.broadcasted_iota(jnp.int32, (frames, pix, chans), 2)
    position = (first * pix + second) * chans + third
    mixed = seeds.astype(jnp.int32)[:, None, None, None] * jnp.int32(-1640531535) + position[None] * jnp.int32(374761393)
    mixed = mixed ^ mixed >> 13
    mixed = mixed * jnp.int32(668265263)
    mixed = mixed ^ mixed >> 16
    chosen = mixed >> 7 & 1
    return 0.1 * (2 * chosen - 1).astype(jnp.float32)

def temporal(inputs, time_weight):
    frames = inputs.shape[1]
    chans = inputs.shape[3]
    padded = jnp.pad(inputs, ((0, 0), (1, 1), (0, 0), (0, 0)))
    result = jnp.zeros(inputs.shape, jnp.float32)
    for k in range(3):
        window = padded[:, k:k + frames].reshape(-1, chans)
        result = result + jnp.dot(window, time_weight[k], preferred_element_type=jnp.float32).reshape(inputs.shape)
    return result

def temporal_back(grad_pre, time_weight):
    frames = grad_pre.shape[1]
    chans = grad_pre.shape[3]
    padded = jnp.pad(grad_pre, ((0, 0), (1, 1), (0, 0), (0, 0)))
    result = jnp.zeros(grad_pre.shape, jnp.float32)
    for k in range(3):
        window = padded[:, 2 - k:2 - k + frames].reshape(-1, chans)
        result = result + jnp.dot(window, time_weight[k].T, preferred_element_type=jnp.float32).reshape(grad_pre.shape)
    return result

def gelu_tanh(value):
    return jax.nn.gelu(value, approximate=True)

def reference(clips, sign_seeds, time_weight, proj_weight, captions, caption_rows):
    frames, pix, chans = (clips.shape[1], clips.shape[2], clips.shape[3])
    delta0 = sign_field(sign_seeds, frames, pix, chans)
    inputs = (clips.astype(jnp.float32) + delta0).astype(jnp.bfloat16)
    pre = temporal(inputs, time_weight)
    active, act_back = jax.vjp(gelu_tanh, pre)
    pooled = lax.optimization_barrier(jnp.mean(active, axis=(1, 2))).astype(jnp.bfloat16)
    video = jnp.dot(pooled, proj_weight, preferred_element_type=jnp.float32)
    vnorm = jnp.sqrt(lax.optimization_barrier(jnp.sum(video * video, axis=1, keepdims=True)) + 1e-06)
    vunit = video / vnorm
    video_hat = vunit.astype(jnp.bfloat16)
    cap32 = captions.astype(jnp.float32)
    caption_hat = (cap32 / jnp.sqrt(lax.optimization_barrier(jnp.sum(cap32 * cap32, axis=1, keepdims=True)) + 1e-06)).astype(jnp.bfloat16)
    scores = jnp.dot(video_hat, caption_hat.T, preferred_element_type=jnp.float32) * INV_TEMP
    expo = jnp.exp(scores)
    every = jnp.arange(CAPS, dtype=jnp.int32)
    own = lax.optimization_barrier(jnp.sum((caption_rows.astype(jnp.int32)[:, :, None] == every[None, None, :]).astype(jnp.float32), axis=1))
    total = lax.optimization_barrier(jnp.sum(expo, axis=1))
    colsum = lax.optimization_barrier(jnp.sum(expo, axis=0))
    positive = lax.optimization_barrier(jnp.sum(own * expo, axis=1))
    text_part = lax.optimization_barrier(jnp.sum(own * (jnp.log(colsum)[None, :] - scores), axis=1))
    clip_loss = jnp.log(total) - jnp.log(positive) + 0.2 * text_part
    weights = expo.astype(jnp.bfloat16)
    pos_weights = (own * expo).astype(jnp.bfloat16)
    scaled = (caption_hat.astype(jnp.float32) / colsum[:, None]).astype(jnp.bfloat16)
    a_sum = jnp.dot(weights, caption_hat, preferred_element_type=jnp.float32)
    b_sum = jnp.dot(weights, scaled, preferred_element_type=jnp.float32)
    pos_sum = jnp.dot(pos_weights, caption_hat, preferred_element_type=jnp.float32)
    own_sum = jnp.dot(own.astype(jnp.bfloat16), caption_hat, preferred_element_type=jnp.float32)
    grad = INV_TEMP * (a_sum / total[:, None] - pos_sum / positive[:, None] + 0.2 * (b_sum - own_sum))
    grad_video = ((grad - vunit * lax.optimization_barrier(jnp.sum(vunit * grad, axis=1, keepdims=True))) / vnorm).astype(jnp.bfloat16)
    grad_pooled = jnp.dot(grad_video, proj_weight.T, preferred_element_type=jnp.float32)
    spread = jnp.broadcast_to(grad_pooled[:, None, None, :] / (frames * pix), pre.shape)
    grad_pre = act_back(spread)[0].astype(jnp.bfloat16)
    grad_in = temporal_back(grad_pre, time_weight)
    rms = jnp.sqrt(lax.optimization_barrier(jnp.mean(grad_in * grad_in, axis=(1, 2, 3), keepdims=True)) + 1e-06)
    new_delta = (delta0 + grad_in / rms).astype(jnp.bfloat16)
    return (new_delta, clip_loss)
```

```python
import functools

import jax
import jax.numpy as jnp
from jax import lax
from jax.experimental import pallas as pl
from jax.experimental.pallas import tpu as pltpu
from jax.sharding import PartitionSpec as P

INV_TEMP = 1.0 / 0.07
GELU_A = 0.7978845608028654
GELU_B = 0.044715
VMEM_LIMIT = 48 << 20


def sign_rows(seed, first_row, rows, frames, pix, chans):
    row = lax.broadcasted_iota(jnp.int32, (rows, 1), 0) + first_row
    pixel = row // frames
    frame = row - pixel * frames
    start = (frame * pix + pixel) * chans * jnp.int32(374761393) + seed * jnp.int32(-1640531535)
    column = lax.broadcasted_iota(jnp.int32, (1, chans), 1) * jnp.int32(374761393)
    mixed = start + column
    mixed = mixed ^ (mixed >> 13)
    mixed = mixed * jnp.int32(668265263)
    mixed = mixed ^ (mixed >> 16)
    return jnp.where((mixed & 128) != 0, jnp.float32(0.1), jnp.float32(-0.1))


def taps(value, frames):
    rows = value.shape[0]
    frame = lax.broadcasted_iota(jnp.int32, (rows, 1), 0) % frames
    before = jnp.where(frame > 0, pltpu.roll(value, 1, 0), 0.0)
    after = jnp.where(frame < frames - 1, pltpu.roll(value, rows - 1, 0), 0.0)
    return before, after


def forward_kernel(dims, seeds, clips, weight, proj, captions, pack, unit, slope, lhs, pre, joined):
    clip_dev, frames, pix, chans, pad = dims
    real = frames * pix
    for i in range(clip_dev):
        base = i * pad
        x = clips[i].astype(jnp.float32).reshape(real, chans)
        x = x + sign_rows(seeds[i], 0, real, frames, pix, chans)
        x = jnp.concatenate([x, jnp.zeros((pad - real, chans), jnp.float32)], 0)
        x = x.astype(jnp.bfloat16).astype(jnp.float32)
        before, after = taps(x, frames)
        lhs[base : base + pad, 0:chans] = before.astype(jnp.bfloat16)
        lhs[base : base + pad, chans : 2 * chans] = x.astype(jnp.bfloat16)
        lhs[base : base + pad, 2 * chans : 3 * chans] = after.astype(jnp.bfloat16)
    pre[...] = jnp.dot(lhs[...], weight[...], preferred_element_type=jnp.float32)
    sums = []
    for i in range(clip_dev):
        v = pre[i * pad : (i + 1) * pad, :]
        square = v * v
        t = jnp.tanh(GELU_A * v * (1.0 + GELU_B * square))
        half = 0.5 + 0.5 * t
        sums.append(jnp.sum(v * half, axis=0, keepdims=True))
        inner = GELU_A * (1.0 + 3.0 * GELU_B * square)
        slope[i * pad : (i + 1) * pad, :] = (half + 0.5 * v * (1.0 - t * t) * inner).astype(jnp.bfloat16)
    pooled = (jnp.concatenate(sums + sums, 0) * (1.0 / real)).astype(jnp.bfloat16)
    video = jnp.dot(pooled, proj[...], preferred_element_type=jnp.float32)
    vnorm = jnp.sqrt(jnp.sum(video * video, axis=1, keepdims=True) + 1e-06)
    vunit = video / vnorm
    unit[0:8, :] = vunit
    unit[8:16, :] = jnp.broadcast_to(vnorm, vunit.shape)
    cap = captions[...].astype(jnp.float32)
    cap = cap / jnp.sqrt(jnp.sum(cap * cap, axis=1, keepdims=True) + 1e-06)
    caps_dev = cap.shape[0]
    joined[0:caps_dev, :] = cap
    joined[caps_dev : caps_dev + clip_dev, :] = vunit[0:clip_dev]
    pack[...] = joined[...].astype(jnp.bfloat16)


def backward_kernel(dims, seeds, rows, every, unit, slope, weight, proj, out, loss, lhs, colsum):
    clip_dev, frames, pix, chans, pad, caps_dev, blocks = dims
    real = frames * pix
    group = caps_dev + clip_dev
    wide = every.shape[0]
    step = 16 * group
    colsum[...] = jnp.zeros_like(colsum)

    def part(b, carry):
        block = every[pl.ds(pl.multiple_of(b * step, step), step), :]
        s = lax.dot_general(block, every[...], (((1,), (1,)), ((), ())), preferred_element_type=jnp.float32)
        row = lax.broadcasted_iota(jnp.int32, (step, 1), 0) % group
        colsum[...] += jnp.sum(jnp.where(row >= caps_dev, jnp.exp(s * INV_TEMP), 0.0), axis=0, keepdims=True)
        return carry

    lax.fori_loop(0, wide // step, part, 0)
    mine = every[group - 8 : group, :]
    scores = lax.dot_general(mine, every[...], (((1,), (1,)), ((), ())), preferred_element_type=jnp.float32) * INV_TEMP
    column = lax.broadcasted_iota(jnp.int32, (1, wide), 1)
    line = lax.broadcasted_iota(jnp.int32, (8, 1), 0)
    expo = jnp.where(column % group < caps_dev, jnp.exp(scores), 0.0)
    own = jnp.zeros((8, wide), jnp.float32)
    for i in range(clip_dev):
        for c in range(rows.shape[1]):
            local = lax.rem(rows[i, c], caps_dev)
            own = own + jnp.where((line == 8 - clip_dev + i) & (column == local), 1.0, 0.0)
    sums = colsum[...]
    sums = jnp.where(column % group < caps_dev, sums, 1.0)
    total = jnp.sum(expo, axis=1, keepdims=True)
    owned = own * expo
    positive = jnp.sum(owned, axis=1, keepdims=True)
    text = jnp.sum(own * (jnp.log(sums) - scores), axis=1, keepdims=True)
    safe = jnp.where(line >= 8 - clip_dev, positive, 1.0)
    value = jnp.log(total) - jnp.log(safe) + 0.2 * text
    place = lax.broadcasted_iota(jnp.int32, (8, 128), 1) + (8 - clip_dev)
    picked = jnp.sum(jnp.where(place == line, value, 0.0), axis=0, keepdims=True)
    loss[...] = picked[:, 0:clip_dev]
    coef = expo / total - owned / safe + 0.2 * (expo / sums - own)
    grad = INV_TEMP * jnp.dot(coef.astype(jnp.bfloat16), every[...], preferred_element_type=jnp.float32)
    vunit = unit[0:8, :]
    vnorm = unit[8:16, :]
    grad_video = ((grad - vunit * jnp.sum(vunit * grad, axis=1, keepdims=True)) / vnorm).astype(jnp.bfloat16)
    grad_pooled = lax.dot_general(
        grad_video, proj[...], (((1,), (1,)), ((), ())), preferred_element_type=jnp.float32
    ) * (1.0 / real)
    for i in range(clip_dev):
        base = i * pad
        g = grad_pooled[8 - clip_dev + i : 8 - clip_dev + i + 1, :]
        gp = slope[base : base + pad, :].astype(jnp.float32) * g
        keep = lax.broadcasted_iota(jnp.int32, (pad, 1), 0) < real
        gp = jnp.where(keep, gp, 0.0)
        before, after = taps(gp, frames)
        lhs[base : base + pad, 0:chans] = after.astype(jnp.bfloat16)
        lhs[base : base + pad, chans : 2 * chans] = gp.astype(jnp.bfloat16)
        lhs[base : base + pad, 2 * chans : 3 * chans] = before.astype(jnp.bfloat16)
    for i in range(clip_dev):
        base = i * pad
        acc = jnp.zeros((pad, chans), jnp.float32)
        for k in range(3):
            acc = acc + lax.dot_general(
                lhs[base : base + pad, k * chans : (k + 1) * chans],
                weight[k],
                (((1,), (1,)), ((), ())),
                preferred_element_type=jnp.float32,
            )
        scale = lax.rsqrt(jnp.sum(acc * acc) / (real * chans) + 1e-06)
        delta = sign_rows(seeds[i], 0, pad, frames, pix, chans) + acc * scale
        out[i] = delta[0:real].reshape(pix, frames, chans).astype(jnp.bfloat16)


def exchange(pack, blocks):
    held = pack
    step = blocks // 2
    while step:
        pairs = [(i, i ^ step) for i in range(blocks)]
        held = jnp.concatenate([held, lax.ppermute(held, "dp", pairs)], 0)
        step //= 2
    return held


def shards(blocks, clips, sign_seeds, time_weight, proj_weight, captions, caption_rows):
    clip_dev, frames, pix, chans = clips.shape
    caps_dev, embed = captions.shape
    pad = -(-frames * pix // 16) * 16
    vmem = pl.BlockSpec(memory_space=pltpu.VMEM)
    smem = pl.BlockSpec(memory_space=pltpu.SMEM)
    params = pltpu.CompilerParams(vmem_limit_bytes=VMEM_LIMIT)
    group = caps_dev + clip_dev
    pack, unit, slope = pl.pallas_call(
        functools.partial(forward_kernel, (clip_dev, frames, pix, chans, pad)),
        out_shape=(
            jax.ShapeDtypeStruct((group, embed), jnp.bfloat16),
            jax.ShapeDtypeStruct((16, embed), jnp.float32),
            jax.ShapeDtypeStruct((clip_dev * pad, chans), jnp.bfloat16),
        ),
        in_specs=[smem, vmem, vmem, vmem, vmem],
        out_specs=(vmem, vmem, vmem),
        scratch_shapes=[
            pltpu.VMEM((clip_dev * pad, 3 * chans), jnp.bfloat16),
            pltpu.VMEM((clip_dev * pad, chans), jnp.float32),
            pltpu.VMEM((group, embed), jnp.float32),
        ],
        compiler_params=params,
        name="forward",
    )(
        sign_seeds,
        clips.transpose(0, 2, 1, 3),
        time_weight.reshape(3 * chans, chans),
        proj_weight,
        captions,
    )
    every = exchange(pack, blocks)
    delta, loss = pl.pallas_call(
        functools.partial(backward_kernel, (clip_dev, frames, pix, chans, pad, caps_dev, blocks)),
        out_shape=(
            jax.ShapeDtypeStruct((clip_dev, pix, frames, chans), jnp.bfloat16),
            jax.ShapeDtypeStruct((1, clip_dev), jnp.float32),
        ),
        in_specs=[smem, smem, vmem, vmem, vmem, vmem, vmem],
        out_specs=(vmem, vmem),
        scratch_shapes=[
            pltpu.VMEM((clip_dev * pad, 3 * chans), jnp.bfloat16),
            pltpu.VMEM((1, blocks * group), jnp.float32),
        ],
        compiler_params=params,
        name="backward",
    )(sign_seeds, caption_rows, every, unit, slope, time_weight, proj_weight)
    return delta.transpose(0, 2, 1, 3), loss.reshape(clip_dev)


def solution(mesh):
    in_specs = (
        P(("groups", "dp"), None, None, None),
        P(("groups", "dp")),
        P(),
        P(),
        P(("groups", "dp"), None),
        P(("groups", "dp"), None),
    )
    out_specs = (P(("groups", "dp"), None, None, None), P(("groups", "dp")))
    return jax.shard_map(
        functools.partial(shards, mesh.shape["dp"]),
        mesh=mesh,
        in_specs=in_specs,
        out_specs=out_specs,
        check_vma=False,
    )
```

```python
import functools

import jax
import jax.numpy as jnp
from jax import lax
from jax.experimental import pallas as pl
from jax.experimental.pallas import tpu as pltpu
from jax.sharding import PartitionSpec as P

INV_TEMP = 1.0 / 0.07
GELU_A = 0.7978845608028654
GELU_B = 0.044715
VMEM_LIMIT = 28 << 20
SLOPE_LIMIT = 8 << 20


def sign_rows(seed, first_row, rows, frames, pix, chans):
    row = lax.broadcasted_iota(jnp.int32, (rows, 1), 0) + first_row
    pixel = row // frames
    frame = row - pixel * frames
    start = (frame * pix + pixel) * chans * jnp.int32(374761393) + seed * jnp.int32(-1640531535)
    column = lax.broadcasted_iota(jnp.int32, (1, chans), 1) * jnp.int32(374761393)
    mixed = start + column
    mixed = mixed ^ (mixed >> 13)
    mixed = mixed * jnp.int32(668265263)
    mixed = mixed ^ (mixed >> 16)
    return jnp.where((mixed & 128) != 0, jnp.float32(0.1), jnp.float32(-0.1))


def clip_of(shape, dim, slot, clip_dev):
    row = lax.broadcasted_iota(jnp.int32, shape, dim)
    return jnp.where(row % slot < slot - 1, row // slot, clip_dev)


def exact_dot(a, b):
    return jnp.dot(a, b, preferred_element_type=jnp.float32, precision=lax.Precision.HIGHEST)


def forward_kernel(
    dims, seeds_hbm, clips_hbm, weight_hbm, proj_hbm, captions_hbm, pack, unit, pre,
    seeds, clips, weight, proj, captions, natural, lhs, joined, sems,
):
    clip_dev, frames, pix, chans, slot = dims
    real, padded, block = frames * pix, frames * slot, clip_dev * slot
    caps_dev = captions.shape[0]
    copies = [pltpu.make_async_copy(seeds_hbm, seeds, sems.at[0])]
    copies += [pltpu.make_async_copy(clips_hbm.at[i], clips.at[i], sems.at[1 + i]) for i in range(clip_dev)]
    copies += [pltpu.make_async_copy(captions_hbm, captions, sems.at[1 + clip_dev])]
    copies += [pltpu.make_async_copy(weight_hbm.at[k], weight.at[k], sems.at[2 + clip_dev + k]) for k in (1, 0, 2)]
    copies += [pltpu.make_async_copy(proj_hbm, proj, sems.at[5 + clip_dev])]
    for copy in copies:
        copy.start()
    copies[0].wait()
    for i in range(clip_dev):
        copies[1 + i].wait()
        x = clips[i].astype(jnp.float32).reshape(real, chans)
        x = x + sign_rows(seeds[i], 0, real, frames, pix, chans)
        for j in range(chans // 128):
            natural[j, i * padded : i * padded + real, :] = x[:, j * 128 : (j + 1) * 128]
            natural[j, i * padded + real : (i + 1) * padded, :] = jnp.zeros((padded - real, 128), jnp.float32)
    for f in range(frames):
        for j in range(chans // 128):
            lhs[f * block : (f + 1) * block, j * 128 : (j + 1) * 128] = natural[
                j, pl.ds(f, block, stride=frames), :
            ].astype(jnp.bfloat16)
    copies[1 + clip_dev].wait()
    cap = captions[...].astype(jnp.float32)
    cap = cap / jnp.sqrt(jnp.sum(cap * cap, axis=1, keepdims=True) + 1e-06)
    joined[0:caps_dev, :] = cap
    rest = (frames - 1) * block
    copies[2 + clip_dev].wait()
    pre[...] = jnp.dot(lhs[...], weight[1], preferred_element_type=jnp.float32)
    copies[3 + clip_dev].wait()
    pre[block:, :] += jnp.dot(lhs[0:rest, :], weight[0], preferred_element_type=jnp.float32)
    copies[4 + clip_dev].wait()
    pre[0:rest, :] += jnp.dot(lhs[block:, :], weight[2], preferred_element_type=jnp.float32)
    active = jnp.zeros((block, chans), jnp.float32)
    for f in range(frames):
        v = pre[f * block : (f + 1) * block, :]
        active = active + v * (0.5 + 0.5 * jnp.tanh(GELU_A * v * (1.0 + GELU_B * (v * v))))
    line = lax.broadcasted_iota(jnp.int32, (8, block), 0) % clip_dev
    belongs = (clip_of((8, block), 1, slot, clip_dev) == line).astype(jnp.float32)
    pooled = (exact_dot(belongs, active) * (1.0 / real)).astype(jnp.bfloat16)
    copies[5 + clip_dev].wait()
    video = jnp.dot(pooled, proj[...], preferred_element_type=jnp.float32)
    vnorm = jnp.sqrt(jnp.sum(video * video, axis=1, keepdims=True) + 1e-06)
    vunit = video / vnorm
    unit[0:8, :] = vunit
    unit[8:16, :] = jnp.broadcast_to(vnorm, vunit.shape)
    joined[caps_dev : caps_dev + clip_dev, :] = vunit[0:clip_dev]
    pack[...] = joined[...].astype(jnp.bfloat16)


def slope_kernel(pre, slope):
    v = pre[...]
    square = v * v
    t = jnp.tanh(GELU_A * v * (1.0 + GELU_B * square))
    inner = GELU_A * (1.0 + 3.0 * GELU_B * square)
    slope[...] = (0.5 + 0.5 * t + 0.5 * v * (1.0 - t * t) * inner).astype(jnp.bfloat16)


def backward_kernel(
    dims, seeds, rows, every, unit, slope, weight, proj, out_hbm, loss, out, lhs, acc, natural, colsum, sems,
):
    clip_dev, frames, pix, chans, slot, caps_dev = dims
    real, padded, block = frames * pix, frames * slot, clip_dev * slot
    group = caps_dev + clip_dev
    wide = every.shape[0]
    step = 16 * group
    colsum[...] = jnp.zeros_like(colsum)

    def part(b, carry):
        chunk = every[pl.ds(pl.multiple_of(b * step, step), step), :]
        s = lax.dot_general(chunk, every[...], (((1,), (1,)), ((), ())), preferred_element_type=jnp.float32)
        row = lax.broadcasted_iota(jnp.int32, (step, 1), 0) % group
        colsum[...] += jnp.sum(jnp.where(row >= caps_dev, jnp.exp(s * INV_TEMP), 0.0), axis=0, keepdims=True)
        return carry

    lax.fori_loop(0, wide // step, part, 0)
    mine = every[group - 8 : group, :]
    scores = lax.dot_general(mine, every[...], (((1,), (1,)), ((), ())), preferred_element_type=jnp.float32) * INV_TEMP
    column = lax.broadcasted_iota(jnp.int32, (1, wide), 1)
    line = lax.broadcasted_iota(jnp.int32, (8, 1), 0)
    expo = jnp.where(column % group < caps_dev, jnp.exp(scores), 0.0)
    own = jnp.zeros((8, wide), jnp.float32)
    for i in range(clip_dev):
        for c in range(rows.shape[1]):
            local = lax.rem(rows[i, c], caps_dev)
            own = own + jnp.where((line == 8 - clip_dev + i) & (column == local), 1.0, 0.0)
    sums = colsum[...]
    sums = jnp.where(column % group < caps_dev, sums, 1.0)
    total = jnp.sum(expo, axis=1, keepdims=True)
    owned = own * expo
    positive = jnp.sum(owned, axis=1, keepdims=True)
    text = jnp.sum(own * (jnp.log(sums) - scores), axis=1, keepdims=True)
    safe = jnp.where(line >= 8 - clip_dev, positive, 1.0)
    value = jnp.log(total) - jnp.log(safe) + 0.2 * text
    place = lax.broadcasted_iota(jnp.int32, (8, 128), 1) + (8 - clip_dev)
    picked = jnp.sum(jnp.where(place == line, value, 0.0), axis=0, keepdims=True)
    loss[...] = picked[:, 0:clip_dev]
    coef = expo / total - owned / safe + 0.2 * (expo / sums - own)
    grad = INV_TEMP * jnp.dot(coef.astype(jnp.bfloat16), every[...], preferred_element_type=jnp.float32)
    vunit = unit[0:8, :]
    vnorm = unit[8:16, :]
    grad_video = ((grad - vunit * jnp.sum(vunit * grad, axis=1, keepdims=True)) / vnorm).astype(jnp.bfloat16)
    grad_pooled = lax.dot_general(
        grad_video, proj[...], (((1,), (1,)), ((), ())), preferred_element_type=jnp.float32
    ) * (1.0 / real)
    line = lax.broadcasted_iota(jnp.int32, (block, 8), 1) - (8 - clip_dev)
    belongs = (clip_of((block, 8), 0, slot, clip_dev) == line).astype(jnp.float32)
    spread = exact_dot(belongs, grad_pooled)
    for f in range(frames):
        part = slice(f * block, (f + 1) * block)
        lhs[part, :] = (slope[part, :].astype(jnp.float32) * spread).astype(jnp.bfloat16)
    rest = (frames - 1) * block
    turned = (((1,), (1,)), ((), ()))
    acc[...] = lax.dot_general(lhs[...], weight[1], turned, preferred_element_type=jnp.float32)
    acc[0:rest, :] += lax.dot_general(lhs[block:, :], weight[0], turned, preferred_element_type=jnp.float32)
    acc[block:, :] += lax.dot_general(lhs[0:rest, :], weight[2], turned, preferred_element_type=jnp.float32)
    squares = jnp.zeros((block, chans), jnp.float32)
    for f in range(frames):
        v = acc[f * block : (f + 1) * block, :]
        squares = squares + v * v
    squares = jnp.sum(squares, axis=1, keepdims=True)
    clip = clip_of((block, 1), 0, slot, clip_dev)
    scale = jnp.zeros((block, 1), jnp.float32)
    for i in range(clip_dev):
        mean = jnp.sum(jnp.where(clip == i, squares, 0.0), axis=0, keepdims=True) * (1.0 / (real * chans))
        scale = jnp.where(clip == i, lax.rsqrt(mean + 1e-06), scale)
    for f in range(frames):
        for j in range(chans // 128):
            part = acc[f * block : (f + 1) * block, j * 128 : (j + 1) * 128]
            natural[j, pl.ds(f, block, stride=frames), :] = part * scale
    copies = []
    for i in range(clip_dev):
        rows_i = slice(i * padded, i * padded + real)
        delta = jnp.concatenate([natural[j, rows_i, :] for j in range(chans // 128)], 1)
        delta = delta + sign_rows(seeds[i], 0, real, frames, pix, chans)
        out[i] = delta.reshape(pix, frames, chans).astype(jnp.bfloat16)
        copies.append(pltpu.make_async_copy(out.at[i], out_hbm.at[i], sems.at[i]))
        copies[-1].start()
    for copy in copies:
        copy.wait()


def exchange(pack, blocks):
    held = pack
    steps = []
    step = blocks // 2
    while step:
        steps.append((step,))
        step //= 2
    if blocks == 16:
        steps = [(8,), (6, 4, 2), (1,)]
    for group in steps:
        parts = [lax.ppermute(held, "dp", [(i, i ^ step) for i in range(blocks)]) for step in group]
        held = jnp.concatenate([held] + parts, 0)
    return held


def shards(blocks, clips, sign_seeds, time_weight, proj_weight, captions, caption_rows):
    clip_dev, frames, pix, chans = clips.shape
    caps_dev, embed = captions.shape
    slot = pix + 1
    total = clip_dev * frames * slot
    group = caps_dev + clip_dev
    vmem = pl.BlockSpec(memory_space=pltpu.VMEM)
    smem = pl.BlockSpec(memory_space=pltpu.SMEM)
    hbm = pl.BlockSpec(memory_space=pltpu.HBM)
    params = pltpu.CompilerParams(vmem_limit_bytes=VMEM_LIMIT)
    pack, unit, pre = pl.pallas_call(
        functools.partial(forward_kernel, (clip_dev, frames, pix, chans, slot)),
        out_shape=(
            jax.ShapeDtypeStruct((group, embed), jnp.bfloat16),
            jax.ShapeDtypeStruct((16, embed), jnp.float32),
            jax.ShapeDtypeStruct((total, chans), jnp.float32),
        ),
        in_specs=[hbm] * 5,
        out_specs=(vmem, vmem, vmem),
        scratch_shapes=[
            pltpu.SMEM((clip_dev,), jnp.int32),
            pltpu.VMEM((clip_dev, pix, frames, chans), jnp.bfloat16),
            pltpu.VMEM((3, chans, chans), jnp.bfloat16),
            pltpu.VMEM((chans, embed), jnp.bfloat16),
            pltpu.VMEM((caps_dev, embed), jnp.bfloat16),
            pltpu.VMEM((chans // 128, total, 128), jnp.float32),
            pltpu.VMEM((total, chans), jnp.bfloat16),
            pltpu.VMEM((group, embed), jnp.float32),
            pltpu.SemaphoreType.DMA((6 + clip_dev,)),
        ],
        compiler_params=params,
        cost_estimate=pl.CostEstimate(flops=6 * total * chans * chans, bytes_accessed=14 << 20, transcendentals=total * chans),
        name="forward",
    )(*[
        pltpu.with_memory_space_constraint(operand, pltpu.HBM)
        for operand in (sign_seeds, clips.transpose(0, 2, 1, 3), time_weight, proj_weight, captions)
    ])
    slope = pl.pallas_call(
        slope_kernel,
        out_shape=jax.ShapeDtypeStruct((total, chans), jnp.bfloat16),
        in_specs=[vmem],
        out_specs=vmem,
        compiler_params=pltpu.CompilerParams(vmem_limit_bytes=SLOPE_LIMIT),
        cost_estimate=pl.CostEstimate(flops=16 * total * chans, bytes_accessed=6 * total * chans, transcendentals=total * chans),
        name="slope",
    )(pre)
    every = exchange(pack, blocks)
    delta, loss = pl.pallas_call(
        functools.partial(backward_kernel, (clip_dev, frames, pix, chans, slot, caps_dev)),
        out_shape=(
            jax.ShapeDtypeStruct((clip_dev, pix, frames, chans), jnp.bfloat16),
            jax.ShapeDtypeStruct((1, clip_dev), jnp.float32),
        ),
        in_specs=[smem, smem, vmem, vmem, vmem, vmem, vmem],
        out_specs=(hbm, vmem),
        scratch_shapes=[
            pltpu.VMEM((clip_dev, pix, frames, chans), jnp.bfloat16),
            pltpu.VMEM((total, chans), jnp.bfloat16),
            pltpu.VMEM((total, chans), jnp.float32),
            pltpu.VMEM((chans // 128, total, 128), jnp.float32),
            pltpu.VMEM((1, blocks * group), jnp.float32),
            pltpu.SemaphoreType.DMA((clip_dev,)),
        ],
        compiler_params=params,
        name="backward",
    )(sign_seeds, caption_rows, every, unit, slope, time_weight, proj_weight)
    return delta.transpose(0, 2, 1, 3), loss.reshape(clip_dev)


def solution(mesh):
    in_specs = (
        P(("groups", "dp"), None, None, None),
        P(("groups", "dp")),
        P(),
        P(),
        P(("groups", "dp"), None),
        P(("groups", "dp"), None),
    )
    out_specs = (P(("groups", "dp"), None, None, None), P(("groups", "dp")))
    return jax.shard_map(
        functools.partial(shards, mesh.shape["dp"]),
        mesh=mesh,
        in_specs=in_specs,
        out_specs=out_specs,
        check_vma=False,
    )
```

```python
import functools

import jax
import jax.numpy as jnp
from jax import lax
from jax.experimental import pallas as pl
from jax.experimental.pallas import tpu as pltpu
from jax.sharding import PartitionSpec as P

INV_TEMP = 1.0 / 0.07
GELU_A = 0.7978845608028654
GELU_B = 0.044715
LANES = 128
CHUNK = 256
HASH_STEP = 374761393
HASH_SEED = -1640531535
HASH_MIX = 668265263


def wrap(value):
    return jnp.int32((value + 2**31) % 2**32 - 2**31)


def signs(mixed):
    mixed = mixed ^ (mixed >> 13)
    mixed = mixed * jnp.int32(HASH_MIX)
    mixed = mixed ^ (mixed >> 16)
    return jnp.where((mixed & 128) != 0, jnp.float32(0.1), jnp.float32(-0.1))


def clip_of(shape, dim, pix, clip_dev):
    return lax.broadcasted_iota(jnp.int32, shape, dim) // pix


def forward_kernel(
    dims, seeds_hbm, rows_hbm, clips_hbm, weight_hbm, proj_hbm, captions_hbm,
    pack, unit, pre, start, own, weight, proj,
    seeds, rows, clips, captions, natural, lhs, active, joined, clip_sems, weight_sems, sems,
):
    clip_dev, frames, pix, chans, block = dims
    dense, tiles = clip_dev * pix, chans // LANES
    caps_dev = captions.shape[0]
    per_chunk = CHUNK // LANES
    small = [
        pltpu.make_async_copy(src, dst, sems.at[i])
        for i, (src, dst) in enumerate(
            [(seeds_hbm, seeds), (rows_hbm, rows), (captions_hbm, captions), (proj_hbm, proj)]
        )
    ]
    clip_copies = [
        pltpu.make_async_copy(clips_hbm.at[:, :, j * LANES : (j + 1) * LANES], clips.at[j], clip_sems.at[j])
        for j in range(tiles)
    ]
    weight_copies = [
        pltpu.make_async_copy(
            weight_hbm.at[:, k * CHUNK : (k + 1) * CHUNK, :],
            weight.at[:, k * CHUNK : (k + 1) * CHUNK, :],
            weight_sems.at[k],
        )
        for k in range(chans // CHUNK)
    ]
    chunks = chans // CHUNK

    def fetch(k):
        for copy in clip_copies[k * per_chunk : (k + 1) * per_chunk]:
            copy.start()
        weight_copies[k].start()

    small[0].start()
    fetch(0)
    for copy in small[1:3]:
        copy.start()
    fetch(1)
    for f in range(frames):
        lhs[f * block + dense : (f + 1) * block, :] = jnp.zeros((block - dense, chans), jnp.bfloat16)
    row = lax.broadcasted_iota(jnp.int32, (dense * frames, LANES), 0)
    spot = row // frames
    clip = spot // pix
    first = ((row % frames) * pix + spot - clip * pix) * chans + lax.broadcasted_iota(jnp.int32, row.shape, 1)
    small[0].wait()
    seed = jnp.zeros(row.shape, jnp.int32)
    for i in range(clip_dev):
        seed = jnp.where(clip == i, seeds[i], seed)
    start[...] = seed * jnp.int32(HASH_SEED) + first * jnp.int32(HASH_STEP)

    def hash_piece(j, rows):
        def run():
            x = clips[j, rows.start // frames : rows.stop // frames].reshape(rows.stop - rows.start, LANES)
            natural[j, rows, :] = x.astype(jnp.float32) + signs(start[rows, :] + wrap(j * LANES * HASH_STEP))

        return run

    def order_piece(j, f):
        def run():
            lhs[f * block : f * block + dense, j * LANES : (j + 1) * LANES] = natural[
                j, pl.ds(f, dense, stride=frames), :
            ].astype(jnp.bfloat16)

        return run

    def prepare(k):
        mine = range(k * per_chunk, (k + 1) * per_chunk)
        for j in mine:
            clip_copies[j].wait()
        length = dense * frames
        cut = next(c for c in (112, 56, 16, length) if length % c == 0)
        pieces = [hash_piece(j, slice(r, r + cut)) for j in mine for r in range(0, length, cut)]
        return pieces + [order_piece(j, f) for j in mine for f in range(frames)]

    def activate(f, columns):
        def run():
            v = pre[f * block : (f + 1) * block, columns]
            gelu = v * (0.5 + 0.5 * jnp.tanh(GELU_A * v * (1.0 + GELU_B * (v * v))))
            active[:, columns] = gelu if f == 0 else active[:, columns] + gelu

        return run

    for piece in prepare(0):
        piece()
    small[1].wait()
    small[2].wait()
    places = [(i, c) for i in range(clip_dev) for c in range(rows.shape[1])]
    base = rows[0, 0]
    for i, c in places:
        base = jnp.minimum(base, rows[i, c])
    line = lax.broadcasted_iota(jnp.int32, own.shape, 0)
    column = lax.broadcasted_iota(jnp.int32, own.shape, 1) + base
    mine = jnp.zeros(own.shape, jnp.float32)
    for i, c in places:
        mine = jnp.where((line == 8 - clip_dev + i) & (column == rows[i, c]), 1.0, mine)
    own[...] = mine
    cap = captions[...].astype(jnp.float32)
    cap = cap / jnp.sqrt(jnp.sum(cap * cap, axis=1, keepdims=True) + 1e-06)
    joined[0:caps_dev, :] = cap
    late = []
    for k in range(chunks):
        weight_copies[k].wait()
        if k + 2 < chunks:
            fetch(k + 2)
        elif k + 2 == chunks:
            small[3].start()
        pieces = prepare(k + 1) if k + 1 < chunks else []
        part = slice(k * CHUNK, (k + 1) * CHUNK)
        products = [(f, n) for n in range(chunks) for f in range(frames)]
        for count, (f, n) in enumerate(products):
            columns = slice(n * CHUNK, (n + 1) * CHUNK)
            taps = [t for t in range(3) if 0 <= f + t - 1 < frames]
            left = jnp.concatenate([lhs[(f + t - 1) * block : (f + t) * block, part] for t in taps], 1)
            right = jnp.concatenate([weight[t, part, columns] for t in taps], 0)
            v = jnp.dot(left, right, preferred_element_type=jnp.float32)
            if k:
                v = v + pre[f * block : (f + 1) * block, columns]
            pre[f * block : (f + 1) * block, columns] = v
            done, todo = len(pieces) * count // len(products), len(pieces) * (count + 1) // len(products)
            for piece in pieces[done:todo]:
                piece()
            if k + 1 == chunks:
                late.append(activate(f, columns))
                if len(late) > 1:
                    late.pop(0)()
    for piece in late:
        piece()
    sums = []
    for i in range(clip_dev):
        low, high = i * pix // 8 * 8, min(-(-(i + 1) * pix // 8) * 8, block)
        row = lax.broadcasted_iota(jnp.int32, (high - low, 1), 0) + low
        inside = (row >= i * pix) & (row < (i + 1) * pix)
        sums.append(jnp.sum(jnp.where(inside, active[low:high, :], 0.0), axis=0, keepdims=True))
    pooled = (jnp.concatenate(sums + sums, 0) * (1.0 / (frames * pix))).astype(jnp.bfloat16)
    small[3].wait()
    video = jnp.dot(pooled, proj[...], preferred_element_type=jnp.float32)
    vnorm = jnp.sqrt(jnp.sum(video * video, axis=1, keepdims=True) + 1e-06)
    vunit = video / vnorm
    unit[0:8, :] = vunit
    unit[8:16, :] = jnp.broadcast_to(vnorm, vunit.shape)
    joined[caps_dev : caps_dev + clip_dev, :] = vunit[0:clip_dev]
    pack[...] = joined[...].astype(jnp.bfloat16)


def slope_kernel(pre, slope):
    v = pre[...]
    square = v * v
    t = jnp.tanh(GELU_A * v * (1.0 + GELU_B * square))
    inner = GELU_A * (1.0 + 3.0 * GELU_B * square)
    slope[...] = (0.5 + 0.5 * t + 0.5 * v * (1.0 - t * t) * inner).astype(jnp.bfloat16)


def delta_kernel(start, delta):
    for j in range(delta.shape[0]):
        delta[j] = signs(start[...] + wrap(j * LANES * HASH_STEP))


def backward_kernel(
    dims, every, unit, own, slope, delta, weight, proj, out_hbm, loss,
    out, lhs, acc, natural, colsum, sems,
):
    clip_dev, frames, pix, chans, block, caps_dev = dims
    dense, tiles = clip_dev * pix, chans // LANES
    real = frames * pix
    group = caps_dev + clip_dev
    wide = every.shape[0]
    step = 16 * group
    colsum[...] = jnp.zeros_like(colsum)

    def part(b, carry):
        chunk = every[pl.ds(pl.multiple_of(b * step, step), step), :]
        s = lax.dot_general(chunk, every[...], (((1,), (1,)), ((), ())), preferred_element_type=jnp.float32)
        row = lax.broadcasted_iota(jnp.int32, (step, 1), 0) % group
        colsum[...] += jnp.sum(jnp.where(row >= caps_dev, jnp.exp(s * INV_TEMP), 0.0), axis=0, keepdims=True)
        return carry

    lax.fori_loop(0, wide // step, part, 0)
    mine = every[group - 8 : group, :]
    scores = lax.dot_general(mine, every[...], (((1,), (1,)), ((), ())), preferred_element_type=jnp.float32) * INV_TEMP
    column = lax.broadcasted_iota(jnp.int32, (1, wide), 1)
    line = lax.broadcasted_iota(jnp.int32, (8, 1), 0)
    expo = jnp.where(column % group < caps_dev, jnp.exp(scores), 0.0)
    owns = jnp.concatenate([own[...], jnp.zeros((8, wide - own.shape[1]), jnp.float32)], 1)
    sums = jnp.where(column % group < caps_dev, colsum[...], 1.0)
    total = jnp.sum(expo, axis=1, keepdims=True)
    owned = owns * expo
    positive = jnp.sum(owned, axis=1, keepdims=True)
    text = jnp.sum(owns * (jnp.log(sums) - scores), axis=1, keepdims=True)
    safe = jnp.where(line >= 8 - clip_dev, positive, 1.0)
    value = jnp.log(total) - jnp.log(safe) + 0.2 * text
    place = lax.broadcasted_iota(jnp.int32, (8, LANES), 1) + (8 - clip_dev)
    picked = jnp.sum(jnp.where(place == line, value, 0.0), axis=0, keepdims=True)
    loss[...] = picked[:, 0:clip_dev]
    coef = expo / total - owned / safe + 0.2 * (expo / sums - owns)
    grad = INV_TEMP * jnp.dot(coef.astype(jnp.bfloat16), every[...], preferred_element_type=jnp.float32)
    vunit = unit[0:8, :]
    vnorm = unit[8:16, :]
    grad_video = ((grad - vunit * jnp.sum(vunit * grad, axis=1, keepdims=True)) / vnorm).astype(jnp.bfloat16)
    grad_pooled = lax.dot_general(
        grad_video, proj[...], (((1,), (1,)), ((), ())), preferred_element_type=jnp.float32
    ) * (1.0 / real)
    clip = clip_of((block, 1), 0, pix, clip_dev)
    spread = jnp.zeros((block, chans), jnp.float32)
    for i in range(clip_dev):
        spread = jnp.where(clip == i, grad_pooled[8 - clip_dev + i : 9 - clip_dev + i, :], spread)
    for f in range(frames):
        rows = slice(f * block, (f + 1) * block)
        lhs[rows, :] = (slope[rows, :].astype(jnp.float32) * spread).astype(jnp.bfloat16)
    rest = (frames - 1) * block
    turned = (((1,), (1,)), ((), ()))
    acc[...] = lax.dot_general(lhs[...], weight[1], turned, preferred_element_type=jnp.float32)
    acc[0:rest, :] += lax.dot_general(lhs[block:, :], weight[0], turned, preferred_element_type=jnp.float32)
    acc[block:, :] += lax.dot_general(lhs[0:rest, :], weight[2], turned, preferred_element_type=jnp.float32)
    squares = jnp.zeros((block, chans), jnp.float32)
    for f in range(frames):
        v = acc[f * block : (f + 1) * block, :]
        squares = squares + v * v
    squares = jnp.sum(squares, axis=1, keepdims=True)
    scale = jnp.zeros((block, 1), jnp.float32)
    for i in range(clip_dev):
        mean = jnp.sum(jnp.where(clip == i, squares, 0.0), axis=0, keepdims=True) * (1.0 / (real * chans))
        scale = jnp.where(clip == i, lax.rsqrt(mean + 1e-06), scale)
    scale = jnp.broadcast_to(scale, (block, LANES))[0:dense]
    copies = []
    for j in range(tiles):
        lanes = slice(j * LANES, (j + 1) * LANES)
        for f in range(frames):
            natural[j, pl.ds(f, dense, stride=frames), :] = acc[f * block : f * block + dense, lanes] * scale
        out[j] = (natural[j] + delta[j]).astype(jnp.bfloat16).reshape(dense, frames, LANES)
        copies.append(pltpu.make_async_copy(out.at[j], out_hbm.at[:, :, lanes], sems.at[j]))
        copies[-1].start()
    for copy in copies:
        copy.wait()


def swap(held, blocks, steps):
    parts = [lax.ppermute(held, "dp", [(i, i ^ step) for i in range(blocks)]) for step in steps]
    return jnp.concatenate([held] + parts, 0)


def shards(blocks, clips, sign_seeds, time_weight, proj_weight, captions, caption_rows):
    clip_dev, frames, pix, chans = clips.shape
    caps_dev, embed = captions.shape
    dense = clip_dev * pix
    block = -(-dense // 8) * 8
    total = frames * block
    group = caps_dev + clip_dev
    tiles = chans // LANES
    bf16, f32, i32 = jnp.bfloat16, jnp.float32, jnp.int32
    shape = jax.ShapeDtypeStruct
    vmem = pl.BlockSpec(memory_space=pltpu.VMEM)
    hbm = pl.BlockSpec(memory_space=pltpu.HBM)
    pack, unit, pre, start, own, weight, proj = pl.pallas_call(
        functools.partial(forward_kernel, (clip_dev, frames, pix, chans, block)),
        out_shape=(
            shape((group, embed), bf16),
            shape((16, embed), f32),
            shape((total, chans), f32),
            shape((dense * frames, LANES), i32),
            shape((8, -(-caps_dev // LANES) * LANES), f32),
            shape((3, chans, chans), bf16),
            shape((chans, embed), bf16),
        ),
        in_specs=[hbm] * 6,
        out_specs=(vmem,) * 7,
        scratch_shapes=[
            pltpu.SMEM((clip_dev,), i32),
            pltpu.SMEM(caption_rows.shape, i32),
            pltpu.VMEM((tiles, dense, frames, LANES), bf16),
            pltpu.VMEM((caps_dev, embed), bf16),
            pltpu.VMEM((tiles, dense * frames, LANES), f32),
            pltpu.VMEM((total, chans), bf16),
            pltpu.VMEM((block, chans), f32),
            pltpu.VMEM((group, embed), f32),
            pltpu.SemaphoreType.DMA((tiles,)),
            pltpu.SemaphoreType.DMA((chans // CHUNK,)),
            pltpu.SemaphoreType.DMA((4,)),
        ],
        compiler_params=pltpu.CompilerParams(vmem_limit_bytes=28 << 20),
        name="forward",
    )(*[
        pltpu.with_memory_space_constraint(operand, pltpu.HBM)
        for operand in (
            sign_seeds,
            caption_rows,
            clips.transpose(0, 2, 1, 3).reshape(dense, frames, chans),
            time_weight,
            proj_weight,
            captions,
        )
    ])
    slope = pl.pallas_call(
        slope_kernel,
        out_shape=shape((total, chans), bf16),
        in_specs=[vmem],
        out_specs=vmem,
        compiler_params=pltpu.CompilerParams(vmem_limit_bytes=8 << 20),
        cost_estimate=pl.CostEstimate(flops=16 * total * chans, bytes_accessed=6 * total * chans, transcendentals=total * chans),
        name="slope",
    )(pre)
    delta = pl.pallas_call(
        delta_kernel,
        out_shape=shape((tiles, dense * frames, LANES), f32),
        in_specs=[vmem],
        out_specs=vmem,
        compiler_params=pltpu.CompilerParams(vmem_limit_bytes=8 << 20),
        cost_estimate=pl.CostEstimate(flops=10 * dense * frames * chans, bytes_accessed=4 * dense * frames * chans, transcendentals=0),
        name="delta",
    )(start)
    if blocks == 16:
        rounds = [(8,), (2, 4, 6), (1,)]
    else:
        rounds = [(1 << b,) for b in reversed(range(blocks.bit_length() - 1))]
    every = pack
    for i, steps in enumerate(rounds):
        every = swap(every, blocks, steps)
        if i == 0:
            every, slope = lax.optimization_barrier((every, slope))
        if i == 1:
            every, delta = lax.optimization_barrier((every, delta))
    out, loss = pl.pallas_call(
        functools.partial(backward_kernel, (clip_dev, frames, pix, chans, block, caps_dev)),
        out_shape=(shape((dense, frames, chans), bf16), shape((1, clip_dev), f32)),
        in_specs=[vmem] * 7,
        out_specs=(hbm, vmem),
        scratch_shapes=[
            pltpu.VMEM((tiles, dense, frames, LANES), bf16),
            pltpu.VMEM((total, chans), bf16),
            pltpu.VMEM((total, chans), f32),
            pltpu.VMEM((tiles, dense * frames, LANES), f32),
            pltpu.VMEM((1, blocks * group), f32),
            pltpu.SemaphoreType.DMA((tiles,)),
        ],
        compiler_params=pltpu.CompilerParams(vmem_limit_bytes=24 << 20),
        name="backward",
    )(every, unit, own, slope, delta, weight, proj)
    out = out.reshape(clip_dev, pix, frames, chans).transpose(0, 2, 1, 3)
    return out, loss.reshape(clip_dev)


def solution(mesh):
    in_specs = (
        P(("groups", "dp"), None, None, None),
        P(("groups", "dp")),
        P(),
        P(),
        P(("groups", "dp"), None),
        P(("groups", "dp"), None),
    )
    out_specs = (P(("groups", "dp"), None, None, None), P(("groups", "dp")))
    return jax.shard_map(
        functools.partial(shards, mesh.shape["dp"]),
        mesh=mesh,
        in_specs=in_specs,
        out_specs=out_specs,
        check_vma=False,
    )
```

```python
import functools

import jax
import jax.numpy as jnp
from jax import lax
from jax.experimental import pallas as pl
from jax.experimental.pallas import tpu as pltpu
from jax.sharding import PartitionSpec as P

INV_TEMP = 1.0 / 0.07
GELU_A = 0.7978845608028654
GELU_B = 0.044715
LANES = 128
CHUNK = 512
TILE = 256
HASH_STEP = 374761393
HASH_SEED = -1640531535
HASH_MIX = 668265263


def wrap(value):
    return jnp.int32((value + 2**31) % 2**32 - 2**31)


def signs(mixed):
    mixed = mixed ^ (mixed >> 13)
    mixed = mixed * jnp.int32(HASH_MIX)
    mixed = mixed ^ (mixed >> 16)
    return jnp.where((mixed & 128) != 0, jnp.float32(0.1), jnp.float32(-0.1))


def clip_of(shape, dim, pix, clip_dev):
    return lax.broadcasted_iota(jnp.int32, shape, dim) // pix


def forward_kernel(
    dims, seeds_hbm, rows_hbm, clips_hbm, weight_hbm, proj_hbm, captions_hbm,
    pack, unit, pre, start, own, weight, proj,
    seeds, rows, clips, captions, natural, lhs, active, joined, clip_sems, weight_sems, sems,
):
    clip_dev, frames, pix, chans, block = dims
    dense, tiles = clip_dev * pix, chans // LANES
    caps_dev = captions.shape[0]
    per_chunk = CHUNK // LANES
    small = [
        pltpu.make_async_copy(src, dst, sems.at[i])
        for i, (src, dst) in enumerate(
            [(seeds_hbm, seeds), (rows_hbm, rows), (captions_hbm, captions), (proj_hbm, proj)]
        )
    ]
    clip_copies = [
        pltpu.make_async_copy(clips_hbm.at[:, :, j * LANES : (j + 1) * LANES], clips.at[j], clip_sems.at[j])
        for j in range(tiles)
    ]
    weight_copies = [
        pltpu.make_async_copy(
            weight_hbm.at[:, k * CHUNK : (k + 1) * CHUNK, :],
            weight.at[:, k * CHUNK : (k + 1) * CHUNK, :],
            weight_sems.at[k],
        )
        for k in range(chans // CHUNK)
    ]
    chunks = chans // CHUNK

    def fetch(k):
        for copy in clip_copies[k * per_chunk : (k + 1) * per_chunk]:
            copy.start()
        weight_copies[k].start()

    small[0].start()
    fetch(0)
    for copy in small[1:3]:
        copy.start()
    fetch(1)
    small[3].start()
    for f in range(frames):
        lhs[f * block + dense : (f + 1) * block, :] = jnp.zeros((block - dense, chans), jnp.bfloat16)
    row = lax.broadcasted_iota(jnp.int32, (dense * frames, LANES), 0)
    spot = row // frames
    clip = spot // pix
    first = ((row % frames) * pix + spot - clip * pix) * chans + lax.broadcasted_iota(jnp.int32, row.shape, 1)
    small[0].wait()
    seed = jnp.zeros(row.shape, jnp.int32)
    for i in range(clip_dev):
        seed = jnp.where(clip == i, seeds[i], seed)
    start[...] = seed * jnp.int32(HASH_SEED) + first * jnp.int32(HASH_STEP)

    def hash_piece(j, rows):
        def run():
            x = clips[j, rows.start // frames : rows.stop // frames].reshape(rows.stop - rows.start, LANES)
            natural[j, rows, :] = x.astype(jnp.float32) + signs(start[rows, :] + wrap(j * LANES * HASH_STEP))

        return run

    def order_piece(j, f):
        def run():
            lhs[f * block : f * block + dense, j * LANES : (j + 1) * LANES] = natural[
                j, pl.ds(f, dense, stride=frames), :
            ].astype(jnp.bfloat16)

        return run

    def prepare(k):
        mine = range(k * per_chunk, (k + 1) * per_chunk)
        for j in mine:
            clip_copies[j].wait()
        length = dense * frames
        cut = next(c for c in (112, 56, 16, length) if length % c == 0)
        pieces = [hash_piece(j, slice(r, r + cut)) for j in mine for r in range(0, length, cut)]
        return pieces + [order_piece(j, f) for j in mine for f in range(frames)]

    def activate(f, columns):
        def run():
            v = pre[f * block : (f + 1) * block, columns]
            gelu = v * (0.5 + 0.5 * jnp.tanh(GELU_A * v * (1.0 + GELU_B * (v * v))))
            active[:, columns] = gelu if f == 0 else active[:, columns] + gelu

        return run

    def project(columns):
        def run():
            sums = []
            for i in range(clip_dev):
                low, high = i * pix // 8 * 8, min(-(-(i + 1) * pix // 8) * 8, block)
                row = lax.broadcasted_iota(jnp.int32, (high - low, 1), 0) + low
                inside = (row >= i * pix) & (row < (i + 1) * pix)
                sums.append(jnp.sum(jnp.where(inside, active[low:high, columns], 0.0), axis=0, keepdims=True))
            pooled = (jnp.concatenate(sums + sums, 0) * (1.0 / (frames * pix))).astype(jnp.bfloat16)
            return jnp.dot(pooled, proj[columns, :], preferred_element_type=jnp.float32)

        return run

    for piece in prepare(0):
        piece()
    small[1].wait()
    small[2].wait()
    places = [(i, c) for i in range(clip_dev) for c in range(rows.shape[1])]
    base = rows[0, 0]
    for i, c in places:
        base = jnp.minimum(base, rows[i, c])
    line = lax.broadcasted_iota(jnp.int32, own.shape, 0)
    column = lax.broadcasted_iota(jnp.int32, own.shape, 1) + base
    mine = jnp.zeros(own.shape, jnp.float32)
    for i, c in places:
        mine = jnp.where((line == 8 - clip_dev + i) & (column == rows[i, c]), 1.0, mine)
    own[...] = mine
    cap = captions[...].astype(jnp.float32)
    cap = cap / jnp.sqrt(jnp.sum(cap * cap, axis=1, keepdims=True) + 1e-06)
    joined[0:caps_dev, :] = cap
    late, parts = [], []
    for k in range(chunks):
        weight_copies[k].wait()
        if k + 2 < chunks:
            fetch(k + 2)
        pieces = prepare(k + 1) if k + 1 < chunks else []
        if k + 1 == chunks:
            small[3].wait()
        part = slice(k * CHUNK, (k + 1) * CHUNK)
        products = [(f, n) for n in range(chans // TILE) for f in range(frames)]
        for count, (f, n) in enumerate(products):
            columns = slice(n * TILE, (n + 1) * TILE)
            taps = [t for t in range(3) if 0 <= f + t - 1 < frames]
            left = jnp.concatenate([lhs[(f + t - 1) * block : (f + t) * block, part] for t in taps], 1)
            right = jnp.concatenate([weight[t, part, columns] for t in taps], 0)
            v = jnp.dot(left, right, preferred_element_type=jnp.float32)
            if k:
                v = v + pre[f * block : (f + 1) * block, columns]
            pre[f * block : (f + 1) * block, columns] = v
            done, todo = len(pieces) * count // len(products), len(pieces) * (count + 1) // len(products)
            for piece in pieces[done:todo]:
                piece()
            if k + 1 == chunks:
                if late:
                    late.pop(0)()
                late.append(activate(f, columns))
                if f == 1 and n:
                    parts.append(project(slice((n - 1) * TILE, n * TILE))())
    late.pop(0)()
    parts.append(project(slice(chans - TILE, chans))())
    video = functools.reduce(lambda a, b: a + b, parts)
    vnorm = jnp.sqrt(jnp.sum(video * video, axis=1, keepdims=True) + 1e-06)
    vunit = video / vnorm
    unit[0:8, :] = vunit
    unit[8:16, :] = jnp.broadcast_to(vnorm, vunit.shape)
    joined[caps_dev : caps_dev + clip_dev, :] = vunit[0:clip_dev]
    pack[...] = joined[...].astype(jnp.bfloat16)


def slope_kernel(pre, slope):
    v = pre[...]
    square = v * v
    t = jnp.tanh(GELU_A * v * (1.0 + GELU_B * square))
    inner = GELU_A * (1.0 + 3.0 * GELU_B * square)
    slope[...] = (0.5 + 0.5 * t + 0.5 * v * (1.0 - t * t) * inner).astype(jnp.bfloat16)


def delta_kernel(start, delta):
    for j in range(delta.shape[0]):
        delta[j] = signs(start[...] + wrap(j * LANES * HASH_STEP))


def backward_kernel(
    dims, every, unit, own, slope, delta, weight, proj, out_hbm, loss,
    out, lhs, acc, natural, colsum, sems,
):
    clip_dev, frames, pix, chans, block, caps_dev = dims
    dense, tiles = clip_dev * pix, chans // LANES
    real = frames * pix
    group = caps_dev + clip_dev
    wide = every.shape[0]
    step = 16 * group
    colsum[...] = jnp.zeros_like(colsum)

    def part(b, carry):
        chunk = every[pl.ds(pl.multiple_of(b * step, step), step), :]
        s = lax.dot_general(chunk, every[...], (((1,), (1,)), ((), ())), preferred_element_type=jnp.float32)
        row = lax.broadcasted_iota(jnp.int32, (step, 1), 0) % group
        colsum[...] += jnp.sum(jnp.where(row >= caps_dev, jnp.exp(s * INV_TEMP), 0.0), axis=0, keepdims=True)
        return carry

    lax.fori_loop(0, wide // step, part, 0)
    mine = every[group - 8 : group, :]
    scores = lax.dot_general(mine, every[...], (((1,), (1,)), ((), ())), preferred_element_type=jnp.float32) * INV_TEMP
    column = lax.broadcasted_iota(jnp.int32, (1, wide), 1)
    line = lax.broadcasted_iota(jnp.int32, (8, 1), 0)
    expo = jnp.where(column % group < caps_dev, jnp.exp(scores), 0.0)
    owns = jnp.concatenate([own[...], jnp.zeros((8, wide - own.shape[1]), jnp.float32)], 1)
    sums = jnp.where(column % group < caps_dev, colsum[...], 1.0)
    total = jnp.sum(expo, axis=1, keepdims=True)
    owned = owns * expo
    positive = jnp.sum(owned, axis=1, keepdims=True)
    text = jnp.sum(owns * (jnp.log(sums) - scores), axis=1, keepdims=True)
    safe = jnp.where(line >= 8 - clip_dev, positive, 1.0)
    value = jnp.log(total) - jnp.log(safe) + 0.2 * text
    place = lax.broadcasted_iota(jnp.int32, (8, LANES), 1) + (8 - clip_dev)
    picked = jnp.sum(jnp.where(place == line, value, 0.0), axis=0, keepdims=True)
    loss[...] = picked[:, 0:clip_dev]
    coef = expo / total - owned / safe + 0.2 * (expo / sums - owns)
    grad = INV_TEMP * jnp.dot(coef.astype(jnp.bfloat16), every[...], preferred_element_type=jnp.float32)
    vunit = unit[0:8, :]
    vnorm = unit[8:16, :]
    grad_video = ((grad - vunit * jnp.sum(vunit * grad, axis=1, keepdims=True)) / vnorm).astype(jnp.bfloat16)
    grad_pooled = lax.dot_general(
        grad_video, proj[...], (((1,), (1,)), ((), ())), preferred_element_type=jnp.float32
    ) * (1.0 / real)
    clip = clip_of((block, 1), 0, pix, clip_dev)
    spread = jnp.zeros((block, chans), jnp.float32)
    for i in range(clip_dev):
        spread = jnp.where(clip == i, grad_pooled[8 - clip_dev + i : 9 - clip_dev + i, :], spread)
    for f in range(frames):
        rows = slice(f * block, (f + 1) * block)
        lhs[rows, :] = (slope[rows, :].astype(jnp.float32) * spread).astype(jnp.bfloat16)
    rest = (frames - 1) * block
    turned = (((1,), (1,)), ((), ()))
    acc[...] = lax.dot_general(lhs[...], weight[1], turned, preferred_element_type=jnp.float32)
    acc[0:rest, :] += lax.dot_general(lhs[block:, :], weight[0], turned, preferred_element_type=jnp.float32)
    acc[block:, :] += lax.dot_general(lhs[0:rest, :], weight[2], turned, preferred_element_type=jnp.float32)
    squares = jnp.zeros((block, chans), jnp.float32)
    for f in range(frames):
        v = acc[f * block : (f + 1) * block, :]
        squares = squares + v * v
    squares = jnp.sum(squares, axis=1, keepdims=True)
    scale = jnp.zeros((block, 1), jnp.float32)
    for i in range(clip_dev):
        mean = jnp.sum(jnp.where(clip == i, squares, 0.0), axis=0, keepdims=True) * (1.0 / (real * chans))
        scale = jnp.where(clip == i, lax.rsqrt(mean + 1e-06), scale)
    scale = jnp.broadcast_to(scale, (block, LANES))[0:dense]
    for j in range(tiles):
        lanes = slice(j * LANES, (j + 1) * LANES)
        for f in range(frames):
            natural[j, pl.ds(f, dense, stride=frames), :] = acc[f * block : f * block + dense, lanes] * scale
    copies = []
    for low in range(0, dense, 56):
        high = min(low + 56, dense)
        rows = slice(low * frames, high * frames)
        for j in range(tiles):
            value = (natural[j, rows, :] + delta[j, rows, :]).astype(jnp.bfloat16)
            out[low:high, :, j * LANES : (j + 1) * LANES] = value.reshape(high - low, frames, LANES)
        copies.append(pltpu.make_async_copy(out.at[low:high], out_hbm.at[low:high], sems.at[low // 56]))
        copies[-1].start()
    for copy in copies:
        copy.wait()


def swap(held, blocks, steps):
    parts = [lax.ppermute(held, "dp", [(i, i ^ step) for i in range(blocks)]) for step in steps]
    return jnp.concatenate([held] + parts, 0)


def shards(blocks, clips, sign_seeds, time_weight, proj_weight, captions, caption_rows):
    clip_dev, frames, pix, chans = clips.shape
    caps_dev, embed = captions.shape
    dense = clip_dev * pix
    block = -(-dense // 8) * 8
    total = frames * block
    group = caps_dev + clip_dev
    tiles = chans // LANES
    bf16, f32, i32 = jnp.bfloat16, jnp.float32, jnp.int32
    shape = jax.ShapeDtypeStruct
    vmem = pl.BlockSpec(memory_space=pltpu.VMEM)
    hbm = pl.BlockSpec(memory_space=pltpu.HBM)
    pack, unit, pre, start, own, weight, proj = pl.pallas_call(
        functools.partial(forward_kernel, (clip_dev, frames, pix, chans, block)),
        out_shape=(
            shape((group, embed), bf16),
            shape((16, embed), f32),
            shape((total, chans), f32),
            shape((dense * frames, LANES), i32),
            shape((8, -(-caps_dev // LANES) * LANES), f32),
            shape((3, chans, chans), bf16),
            shape((chans, embed), bf16),
        ),
        in_specs=[hbm] * 6,
        out_specs=(vmem,) * 7,
        scratch_shapes=[
            pltpu.SMEM((clip_dev,), i32),
            pltpu.SMEM(caption_rows.shape, i32),
            pltpu.VMEM((tiles, dense, frames, LANES), bf16),
            pltpu.VMEM((caps_dev, embed), bf16),
            pltpu.VMEM((tiles, dense * frames, LANES), f32),
            pltpu.VMEM((total, chans), bf16),
            pltpu.VMEM((block, chans), f32),
            pltpu.VMEM((group, embed), f32),
            pltpu.SemaphoreType.DMA((tiles,)),
            pltpu.SemaphoreType.DMA((chans // CHUNK,)),
            pltpu.SemaphoreType.DMA((4,)),
        ],
        compiler_params=pltpu.CompilerParams(vmem_limit_bytes=28 << 20),
        name="forward",
    )(*[
        pltpu.with_memory_space_constraint(operand, pltpu.HBM)
        for operand in (
            sign_seeds,
            caption_rows,
            clips.transpose(0, 2, 1, 3).reshape(dense, frames, chans),
            time_weight,
            proj_weight,
            captions,
        )
    ])
    slope = pl.pallas_call(
        slope_kernel,
        out_shape=shape((total, chans), bf16),
        in_specs=[vmem],
        out_specs=vmem,
        compiler_params=pltpu.CompilerParams(vmem_limit_bytes=8 << 20),
        cost_estimate=pl.CostEstimate(flops=16 * total * chans, bytes_accessed=6 * total * chans, transcendentals=total * chans),
        name="slope",
    )(pre)
    delta = pl.pallas_call(
        delta_kernel,
        out_shape=shape((tiles, dense * frames, LANES), f32),
        in_specs=[vmem],
        out_specs=vmem,
        compiler_params=pltpu.CompilerParams(vmem_limit_bytes=8 << 20),
        cost_estimate=pl.CostEstimate(flops=10 * dense * frames * chans, bytes_accessed=4 * dense * frames * chans, transcendentals=0),
        name="delta",
    )(start)
    if blocks == 16:
        rounds = [(8,), (2, 4, 6), (1,)]
    else:
        rounds = [(1 << b,) for b in reversed(range(blocks.bit_length() - 1))]
    every = pack
    for i, steps in enumerate(rounds):
        every = swap(every, blocks, steps)
        if i == 0:
            every, delta = lax.optimization_barrier((every, delta))
        if i == 1:
            every, slope = lax.optimization_barrier((every, slope))
    out, loss = pl.pallas_call(
        functools.partial(backward_kernel, (clip_dev, frames, pix, chans, block, caps_dev)),
        out_shape=(shape((dense, frames, chans), bf16), shape((1, clip_dev), f32)),
        in_specs=[vmem] * 7,
        out_specs=(hbm, vmem),
        scratch_shapes=[
            pltpu.VMEM((dense, frames, chans), bf16),
            pltpu.VMEM((total, chans), bf16),
            pltpu.VMEM((total, chans), f32),
            pltpu.VMEM((tiles, dense * frames, LANES), f32),
            pltpu.VMEM((1, blocks * group), f32),
            pltpu.SemaphoreType.DMA((-(-dense // 56),)),
        ],
        compiler_params=pltpu.CompilerParams(vmem_limit_bytes=24 << 20),
        name="backward",
    )(every, unit, own, slope, delta, weight, proj)
    out = out.reshape(clip_dev, pix, frames, chans).transpose(0, 2, 1, 3)
    return out, loss.reshape(clip_dev)


def solution(mesh):
    in_specs = (
        P(("groups", "dp"), None, None, None),
        P(("groups", "dp")),
        P(),
        P(),
        P(("groups", "dp"), None),
        P(("groups", "dp"), None),
    )
    out_specs = (P(("groups", "dp"), None, None, None), P(("groups", "dp")))
    return jax.shard_map(
        functools.partial(shards, mesh.shape["dp"]),
        mesh=mesh,
        in_specs=in_specs,
        out_specs=out_specs,
        check_vma=False,
    )
```

```python
import functools

import jax
import jax.numpy as jnp
from jax import lax
from jax.experimental import pallas as pl
from jax.experimental.pallas import tpu as pltpu
from jax.sharding import PartitionSpec as P

INV_TEMP = 1.0 / 0.07
GELU_A = 0.7978845608028654
GELU_B = 0.044715
LANES = 128
CHUNK = 512
TILE = 256
HASH_STEP = 374761393
HASH_SEED = -1640531535
HASH_MIX = 668265263


def wrap(value):
    return jnp.int32((value + 2**31) % 2**32 - 2**31)


def signs(mixed):
    mixed = mixed ^ (mixed >> 13)
    mixed = mixed * jnp.int32(HASH_MIX)
    mixed = mixed ^ (mixed >> 16)
    return jnp.where((mixed & 128) != 0, jnp.float32(0.1), jnp.float32(-0.1))


def clip_of(shape, dim, pix, clip_dev):
    return lax.broadcasted_iota(jnp.int32, shape, dim) // pix


def forward_kernel(
    dims, seeds_hbm, rows_hbm, clips_hbm, weight_hbm, proj_hbm, captions_hbm,
    pack, unit, pre, delta, own, weight, proj,
    start, seeds, rows, clips, captions, natural, lhs, active, joined, clip_sems, weight_sems, sems,
):
    clip_dev, frames, pix, chans, block = dims
    dense, tiles = clip_dev * pix, chans // LANES
    caps_dev = captions.shape[0]
    per_chunk = CHUNK // LANES
    small = [
        pltpu.make_async_copy(src, dst, sems.at[i])
        for i, (src, dst) in enumerate(
            [(seeds_hbm, seeds), (rows_hbm, rows), (captions_hbm, captions), (proj_hbm, proj)]
        )
    ]
    clip_copies = [
        pltpu.make_async_copy(clips_hbm.at[:, :, j * LANES : (j + 1) * LANES], clips.at[j], clip_sems.at[j])
        for j in range(tiles)
    ]
    weight_copies = [
        pltpu.make_async_copy(
            weight_hbm.at[:, k * CHUNK : (k + 1) * CHUNK, :],
            weight.at[:, k * CHUNK : (k + 1) * CHUNK, :],
            weight_sems.at[k],
        )
        for k in range(chans // CHUNK)
    ]
    chunks = chans // CHUNK

    def fetch(k):
        for copy in clip_copies[k * per_chunk : (k + 1) * per_chunk]:
            copy.start()
        weight_copies[k].start()

    small[0].start()
    fetch(0)
    for copy in small[1:3]:
        copy.start()
    fetch(1)
    small[3].start()
    for f in range(frames):
        lhs[f * block + dense : (f + 1) * block, :] = jnp.zeros((block - dense, chans), jnp.bfloat16)
    row = lax.broadcasted_iota(jnp.int32, (dense * frames, LANES), 0)
    spot = row // frames
    clip = spot // pix
    first = ((row % frames) * pix + spot - clip * pix) * chans + lax.broadcasted_iota(jnp.int32, row.shape, 1)
    small[0].wait()
    seed = jnp.zeros(row.shape, jnp.int32)
    for i in range(clip_dev):
        seed = jnp.where(clip == i, seeds[i], seed)
    start[...] = seed * jnp.int32(HASH_SEED) + first * jnp.int32(HASH_STEP)
    for j in range(tiles):
        delta[j] = signs(start[...] + wrap(j * LANES * HASH_STEP))

    def hash_piece(j, rows):
        def run():
            x = clips[j, rows.start // frames : rows.stop // frames].reshape(rows.stop - rows.start, LANES)
            natural[j, rows, :] = x.astype(jnp.float32) + delta[j, rows, :]

        return run

    def order_piece(j, f):
        def run():
            lhs[f * block : f * block + dense, j * LANES : (j + 1) * LANES] = natural[
                j, pl.ds(f, dense, stride=frames), :
            ].astype(jnp.bfloat16)

        return run

    def prepare(k):
        mine = range(k * per_chunk, (k + 1) * per_chunk)
        for j in mine:
            clip_copies[j].wait()
        length = dense * frames
        cut = next(c for c in (112, 56, 16, length) if length % c == 0)
        pieces = [hash_piece(j, slice(r, r + cut)) for j in mine for r in range(0, length, cut)]
        return pieces + [order_piece(j, f) for j in mine for f in range(frames)]

    def activate(f, columns):
        def run():
            v = pre[f * block : (f + 1) * block, columns]
            gelu = v * (0.5 + 0.5 * jnp.tanh(GELU_A * v * (1.0 + GELU_B * (v * v))))
            active[:, columns] = gelu if f == 0 else active[:, columns] + gelu

        return run

    def project(columns):
        def run():
            sums = []
            for i in range(clip_dev):
                low, high = i * pix // 8 * 8, min(-(-(i + 1) * pix // 8) * 8, block)
                row = lax.broadcasted_iota(jnp.int32, (high - low, 1), 0) + low
                inside = (row >= i * pix) & (row < (i + 1) * pix)
                sums.append(jnp.sum(jnp.where(inside, active[low:high, columns], 0.0), axis=0, keepdims=True))
            pooled = (jnp.concatenate(sums + sums, 0) * (1.0 / (frames * pix))).astype(jnp.bfloat16)
            return jnp.dot(pooled, proj[columns, :], preferred_element_type=jnp.float32)

        return run

    for piece in prepare(0):
        piece()
    small[1].wait()
    small[2].wait()
    places = [(i, c) for i in range(clip_dev) for c in range(rows.shape[1])]
    base = rows[0, 0]
    for i, c in places:
        base = jnp.minimum(base, rows[i, c])
    line = lax.broadcasted_iota(jnp.int32, own.shape, 0)
    column = lax.broadcasted_iota(jnp.int32, own.shape, 1) + base
    mine = jnp.zeros(own.shape, jnp.float32)
    for i, c in places:
        mine = jnp.where((line == 8 - clip_dev + i) & (column == rows[i, c]), 1.0, mine)
    own[...] = mine
    cap = captions[...].astype(jnp.float32)
    cap = cap / jnp.sqrt(jnp.sum(cap * cap, axis=1, keepdims=True) + 1e-06)
    joined[0:caps_dev, :] = cap
    late, parts = [], []
    for k in range(chunks):
        weight_copies[k].wait()
        if k + 2 < chunks:
            fetch(k + 2)
        pieces = prepare(k + 1) if k + 1 < chunks else []
        if k + 1 == chunks:
            small[3].wait()
        part = slice(k * CHUNK, (k + 1) * CHUNK)
        products = [(f, n) for n in range(chans // TILE) for f in range(frames)]
        for count, (f, n) in enumerate(products):
            columns = slice(n * TILE, (n + 1) * TILE)
            taps = [t for t in range(3) if 0 <= f + t - 1 < frames]
            left = jnp.concatenate([lhs[(f + t - 1) * block : (f + t) * block, part] for t in taps], 1)
            right = jnp.concatenate([weight[t, part, columns] for t in taps], 0)
            v = jnp.dot(left, right, preferred_element_type=jnp.float32)
            if k:
                v = v + pre[f * block : (f + 1) * block, columns]
            pre[f * block : (f + 1) * block, columns] = v
            done, todo = len(pieces) * count // len(products), len(pieces) * (count + 1) // len(products)
            for piece in pieces[done:todo]:
                piece()
            if k + 1 == chunks:
                if late:
                    late.pop(0)()
                late.append(activate(f, columns))
                if f == 1 and n:
                    parts.append(project(slice((n - 1) * TILE, n * TILE))())
    late.pop(0)()
    parts.append(project(slice(chans - TILE, chans))())
    video = functools.reduce(lambda a, b: a + b, parts)
    vnorm = jnp.sqrt(jnp.sum(video * video, axis=1, keepdims=True) + 1e-06)
    vunit = video / vnorm
    unit[0:8, :] = vunit
    unit[8:16, :] = jnp.broadcast_to(vnorm, vunit.shape)
    joined[caps_dev : caps_dev + clip_dev, :] = vunit[0:clip_dev]
    pack[...] = joined[...].astype(jnp.bfloat16)


def slope_kernel(pre, slope):
    v = pre[...]
    square = v * v
    t = jnp.tanh(GELU_A * v * (1.0 + GELU_B * square))
    inner = GELU_A * (1.0 + 3.0 * GELU_B * square)
    slope[...] = (0.5 + 0.5 * t + 0.5 * v * (1.0 - t * t) * inner).astype(jnp.bfloat16)


def backward_kernel(
    dims, every, unit, own, slope, delta, weight, proj, out_hbm, loss,
    out, lhs, acc, natural, colsum, sems,
):
    clip_dev, frames, pix, chans, block, caps_dev = dims
    dense, tiles = clip_dev * pix, chans // LANES
    real = frames * pix
    group = caps_dev + clip_dev
    wide = every.shape[0]
    step = 16 * group
    colsum[...] = jnp.zeros_like(colsum)

    def part(b, carry):
        chunk = every[pl.ds(pl.multiple_of(b * step, step), step), :]
        s = lax.dot_general(chunk, every[...], (((1,), (1,)), ((), ())), preferred_element_type=jnp.float32)
        row = lax.broadcasted_iota(jnp.int32, (step, 1), 0) % group
        colsum[...] += jnp.sum(jnp.where(row >= caps_dev, jnp.exp(s * INV_TEMP), 0.0), axis=0, keepdims=True)
        return carry

    lax.fori_loop(0, wide // step, part, 0)
    mine = every[group - 8 : group, :]
    scores = lax.dot_general(mine, every[...], (((1,), (1,)), ((), ())), preferred_element_type=jnp.float32) * INV_TEMP
    column = lax.broadcasted_iota(jnp.int32, (1, wide), 1)
    line = lax.broadcasted_iota(jnp.int32, (8, 1), 0)
    expo = jnp.where(column % group < caps_dev, jnp.exp(scores), 0.0)
    owns = jnp.concatenate([own[...], jnp.zeros((8, wide - own.shape[1]), jnp.float32)], 1)
    sums = jnp.where(column % group < caps_dev, colsum[...], 1.0)
    total = jnp.sum(expo, axis=1, keepdims=True)
    owned = owns * expo
    positive = jnp.sum(owned, axis=1, keepdims=True)
    text = jnp.sum(owns * (jnp.log(sums) - scores), axis=1, keepdims=True)
    safe = jnp.where(line >= 8 - clip_dev, positive, 1.0)
    value = jnp.log(total) - jnp.log(safe) + 0.2 * text
    place = lax.broadcasted_iota(jnp.int32, (8, LANES), 1) + (8 - clip_dev)
    picked = jnp.sum(jnp.where(place == line, value, 0.0), axis=0, keepdims=True)
    loss[...] = picked[:, 0:clip_dev]
    coef = expo / total - owned / safe + 0.2 * (expo / sums - owns)
    grad = INV_TEMP * jnp.dot(coef.astype(jnp.bfloat16), every[...], preferred_element_type=jnp.float32)
    vunit = unit[0:8, :]
    vnorm = unit[8:16, :]
    grad_video = ((grad - vunit * jnp.sum(vunit * grad, axis=1, keepdims=True)) / vnorm).astype(jnp.bfloat16)
    grad_pooled = lax.dot_general(
        grad_video, proj[...], (((1,), (1,)), ((), ())), preferred_element_type=jnp.float32
    ) * (1.0 / real)
    clip = clip_of((block, 1), 0, pix, clip_dev)
    spread = jnp.zeros((block, chans), jnp.float32)
    for i in range(clip_dev):
        spread = jnp.where(clip == i, grad_pooled[8 - clip_dev + i : 9 - clip_dev + i, :], spread)
    for f in range(frames):
        rows = slice(f * block, (f + 1) * block)
        lhs[rows, :] = (slope[rows, :].astype(jnp.float32) * spread).astype(jnp.bfloat16)
    rest = (frames - 1) * block
    turned = (((1,), (1,)), ((), ()))
    acc[...] = lax.dot_general(lhs[...], weight[1], turned, preferred_element_type=jnp.float32)
    acc[0:rest, :] += lax.dot_general(lhs[block:, :], weight[0], turned, preferred_element_type=jnp.float32)
    acc[block:, :] += lax.dot_general(lhs[0:rest, :], weight[2], turned, preferred_element_type=jnp.float32)
    squares = jnp.zeros((block, chans), jnp.float32)
    for f in range(frames):
        v = acc[f * block : (f + 1) * block, :]
        squares = squares + v * v
    squares = jnp.sum(squares, axis=1, keepdims=True)
    scale = jnp.zeros((block, 1), jnp.float32)
    for i in range(clip_dev):
        mean = jnp.sum(jnp.where(clip == i, squares, 0.0), axis=0, keepdims=True) * (1.0 / (real * chans))
        scale = jnp.where(clip == i, lax.rsqrt(mean + 1e-06), scale)
    scale = jnp.broadcast_to(scale, (block, LANES))[0:dense]
    for j in range(tiles):
        lanes = slice(j * LANES, (j + 1) * LANES)
        for f in range(frames):
            natural[j, pl.ds(f, dense, stride=frames), :] = acc[f * block : f * block + dense, lanes] * scale
    copies = []
    for low in range(0, dense, 56):
        high = min(low + 56, dense)
        rows = slice(low * frames, high * frames)
        for j in range(tiles):
            value = (natural[j, rows, :] + delta[j, rows, :]).astype(jnp.bfloat16)
            out[low:high, :, j * LANES : (j + 1) * LANES] = value.reshape(high - low, frames, LANES)
        copies.append(pltpu.make_async_copy(out.at[low:high], out_hbm.at[low:high], sems.at[low // 56]))
        copies[-1].start()
    for copy in copies:
        copy.wait()


def swap(held, blocks, steps):
    parts = [lax.ppermute(held, "dp", [(i, i ^ step) for i in range(blocks)]) for step in steps]
    return jnp.concatenate([held] + parts, 0)


def shards(blocks, clips, sign_seeds, time_weight, proj_weight, captions, caption_rows):
    clip_dev, frames, pix, chans = clips.shape
    caps_dev, embed = captions.shape
    dense = clip_dev * pix
    block = -(-dense // 8) * 8
    total = frames * block
    group = caps_dev + clip_dev
    tiles = chans // LANES
    bf16, f32, i32 = jnp.bfloat16, jnp.float32, jnp.int32
    shape = jax.ShapeDtypeStruct
    vmem = pl.BlockSpec(memory_space=pltpu.VMEM)
    hbm = pl.BlockSpec(memory_space=pltpu.HBM)
    pack, unit, pre, delta, own, weight, proj = pl.pallas_call(
        functools.partial(forward_kernel, (clip_dev, frames, pix, chans, block)),
        out_shape=(
            shape((group, embed), bf16),
            shape((16, embed), f32),
            shape((total, chans), f32),
            shape((tiles, dense * frames, LANES), f32),
            shape((8, -(-caps_dev // LANES) * LANES), f32),
            shape((3, chans, chans), bf16),
            shape((chans, embed), bf16),
        ),
        in_specs=[hbm] * 6,
        out_specs=(vmem,) * 7,
        scratch_shapes=[
            pltpu.VMEM((dense * frames, LANES), i32),
            pltpu.SMEM((clip_dev,), i32),
            pltpu.SMEM(caption_rows.shape, i32),
            pltpu.VMEM((tiles, dense, frames, LANES), bf16),
            pltpu.VMEM((caps_dev, embed), bf16),
            pltpu.VMEM((tiles, dense * frames, LANES), f32),
            pltpu.VMEM((total, chans), bf16),
            pltpu.VMEM((block, chans), f32),
            pltpu.VMEM((group, embed), f32),
            pltpu.SemaphoreType.DMA((tiles,)),
            pltpu.SemaphoreType.DMA((chans // CHUNK,)),
            pltpu.SemaphoreType.DMA((4,)),
        ],
        compiler_params=pltpu.CompilerParams(vmem_limit_bytes=28 << 20),
        name="forward",
    )(*[
        pltpu.with_memory_space_constraint(operand, pltpu.HBM)
        for operand in (
            sign_seeds,
            caption_rows,
            clips.transpose(0, 2, 1, 3).reshape(dense, frames, chans),
            time_weight,
            proj_weight,
            captions,
        )
    ])
    slope = pl.pallas_call(
        slope_kernel,
        out_shape=shape((total, chans), bf16),
        in_specs=[vmem],
        out_specs=vmem,
        compiler_params=pltpu.CompilerParams(vmem_limit_bytes=8 << 20),
        cost_estimate=pl.CostEstimate(flops=16 * total * chans, bytes_accessed=6 * total * chans, transcendentals=total * chans),
        name="slope",
    )(pre)
    if blocks == 16:
        rounds = [(8,), (2, 4, 6), (1,)]
    else:
        rounds = [(1 << b,) for b in reversed(range(blocks.bit_length() - 1))]
    every = pack
    for i, steps in enumerate(rounds):
        every = swap(every, blocks, steps)
        if i == 0:
            every, slope = lax.optimization_barrier((every, slope))
    out, loss = pl.pallas_call(
        functools.partial(backward_kernel, (clip_dev, frames, pix, chans, block, caps_dev)),
        out_shape=(shape((dense, frames, chans), bf16), shape((1, clip_dev), f32)),
        in_specs=[vmem] * 7,
        out_specs=(hbm, vmem),
        scratch_shapes=[
            pltpu.VMEM((dense, frames, chans), bf16),
            pltpu.VMEM((total, chans), bf16),
            pltpu.VMEM((total, chans), f32),
            pltpu.VMEM((tiles, dense * frames, LANES), f32),
            pltpu.VMEM((1, blocks * group), f32),
            pltpu.SemaphoreType.DMA((-(-dense // 56),)),
        ],
        compiler_params=pltpu.CompilerParams(vmem_limit_bytes=24 << 20),
        name="backward",
    )(every, unit, own, slope, delta, weight, proj)
    out = out.reshape(clip_dev, pix, frames, chans).transpose(0, 2, 1, 3)
    return out, loss.reshape(clip_dev)


def solution(mesh):
    in_specs = (
        P(("groups", "dp"), None, None, None),
        P(("groups", "dp")),
        P(),
        P(),
        P(("groups", "dp"), None),
        P(("groups", "dp"), None),
    )
    out_specs = (P(("groups", "dp"), None, None, None), P(("groups", "dp")))
    return jax.shard_map(
        functools.partial(shards, mesh.shape["dp"]),
        mesh=mesh,
        in_specs=in_specs,
        out_specs=out_specs,
        check_vma=False,
    )
```

```python
import functools

import jax
import jax.numpy as jnp
from jax import lax
from jax.experimental import pallas as pl
from jax.experimental.pallas import tpu as pltpu
from jax.sharding import PartitionSpec as P

INV_TEMP = 1.0 / 0.07
GELU_A = 0.7978845608028654
GELU_B = 0.044715
LANES = 128
CHUNK = 512
TILE = 512
HASH_STEP = 374761393
HASH_SEED = -1640531535
HASH_MIX = 668265263


def wrap(value):
    return jnp.int32((value + 2**31) % 2**32 - 2**31)


def signs(mixed):
    mixed = mixed ^ (mixed >> 13)
    mixed = mixed * jnp.int32(HASH_MIX)
    mixed = mixed ^ (mixed >> 16)
    return jnp.where((mixed & 128) != 0, jnp.float32(0.1), jnp.float32(-0.1))


def clip_of(shape, dim, pix, clip_dev):
    return lax.broadcasted_iota(jnp.int32, shape, dim) // pix


def forward_kernel(
    dims, seeds_hbm, rows_hbm, clips_hbm, weight_hbm, proj_hbm, captions_hbm,
    pack, unit, pre, delta, own, weight, proj,
    start, seeds, rows, clips, captions, natural, lhs, active, joined, clip_sems, weight_sems, sems,
):
    clip_dev, frames, pix, chans, block = dims
    dense, tiles = clip_dev * pix, chans // LANES
    caps_dev = captions.shape[0]
    per_chunk = CHUNK // LANES
    small = [
        pltpu.make_async_copy(src, dst, sems.at[i])
        for i, (src, dst) in enumerate(
            [(seeds_hbm, seeds), (rows_hbm, rows), (captions_hbm, captions), (proj_hbm, proj)]
        )
    ]
    clip_copies = [
        pltpu.make_async_copy(clips_hbm.at[:, :, j * LANES : (j + 1) * LANES], clips.at[j], clip_sems.at[j])
        for j in range(tiles)
    ]
    weight_copies = [
        pltpu.make_async_copy(
            weight_hbm.at[:, k * CHUNK : (k + 1) * CHUNK, :],
            weight.at[:, k * CHUNK : (k + 1) * CHUNK, :],
            weight_sems.at[k],
        )
        for k in range(chans // CHUNK)
    ]
    chunks = chans // CHUNK

    def fetch(k):
        for copy in clip_copies[k * per_chunk : (k + 1) * per_chunk]:
            copy.start()
        weight_copies[k].start()

    small[0].start()
    fetch(0)
    for copy in small[1:3]:
        copy.start()
    fetch(1)
    small[3].start()
    for f in range(frames):
        lhs[f * block + dense : (f + 1) * block, :] = jnp.zeros((block - dense, chans), jnp.bfloat16)
    row = lax.broadcasted_iota(jnp.int32, (dense * frames, LANES), 0)
    spot = row // frames
    clip = spot // pix
    first = ((row % frames) * pix + spot - clip * pix) * chans + lax.broadcasted_iota(jnp.int32, row.shape, 1)
    small[0].wait()
    seed = jnp.zeros(row.shape, jnp.int32)
    for i in range(clip_dev):
        seed = jnp.where(clip == i, seeds[i], seed)
    start[...] = seed * jnp.int32(HASH_SEED) + first * jnp.int32(HASH_STEP)
    for j in range(tiles):
        delta[j] = signs(start[...] + wrap(j * LANES * HASH_STEP))

    def hash_piece(j, rows):
        def run():
            x = clips[j, rows.start // frames : rows.stop // frames].reshape(rows.stop - rows.start, LANES)
            natural[j, rows, :] = x.astype(jnp.float32) + delta[j, rows, :]

        return run

    def order_piece(j, f):
        def run():
            lhs[f * block : f * block + dense, j * LANES : (j + 1) * LANES] = natural[
                j, pl.ds(f, dense, stride=frames), :
            ].astype(jnp.bfloat16)

        return run

    def prepare(k):
        mine = range(k * per_chunk, (k + 1) * per_chunk)
        for j in mine:
            clip_copies[j].wait()
        length = dense * frames
        cut = next(c for c in (112, 56, 16, length) if length % c == 0)
        pieces = [hash_piece(j, slice(r, r + cut)) for j in mine for r in range(0, length, cut)]
        return pieces + [order_piece(j, f) for j in mine for f in range(frames)]

    def activate(f, columns):
        def run():
            v = pre[f * block : (f + 1) * block, columns]
            gelu = v * (0.5 + 0.5 * jnp.tanh(GELU_A * v * (1.0 + GELU_B * (v * v))))
            active[:, columns] = gelu if f == 0 else active[:, columns] + gelu

        return run

    def project(columns):
        def run():
            sums = []
            for i in range(clip_dev):
                low, high = i * pix // 8 * 8, min(-(-(i + 1) * pix // 8) * 8, block)
                row = lax.broadcasted_iota(jnp.int32, (high - low, 1), 0) + low
                inside = (row >= i * pix) & (row < (i + 1) * pix)
                sums.append(jnp.sum(jnp.where(inside, active[low:high, columns], 0.0), axis=0, keepdims=True))
            pooled = (jnp.concatenate(sums + sums, 0) * (1.0 / (frames * pix))).astype(jnp.bfloat16)
            return jnp.dot(pooled, proj[columns, :], preferred_element_type=jnp.float32)

        return run

    for piece in prepare(0):
        piece()
    small[1].wait()
    small[2].wait()
    places = [(i, c) for i in range(clip_dev) for c in range(rows.shape[1])]
    base = rows[0, 0]
    for i, c in places:
        base = jnp.minimum(base, rows[i, c])
    line = lax.broadcasted_iota(jnp.int32, own.shape, 0)
    column = lax.broadcasted_iota(jnp.int32, own.shape, 1) + base
    mine = jnp.zeros(own.shape, jnp.float32)
    for i, c in places:
        mine = jnp.where((line == 8 - clip_dev + i) & (column == rows[i, c]), 1.0, mine)
    own[...] = mine
    cap = captions[...].astype(jnp.float32)
    cap = cap / jnp.sqrt(jnp.sum(cap * cap, axis=1, keepdims=True) + 1e-06)
    joined[0:caps_dev, :] = cap
    late, parts = [], []
    for k in range(chunks):
        weight_copies[k].wait()
        if k + 2 < chunks:
            fetch(k + 2)
        pieces = prepare(k + 1) if k + 1 < chunks else []
        if k + 1 == chunks:
            small[3].wait()
        part = slice(k * CHUNK, (k + 1) * CHUNK)
        products = [(f, n) for n in range(chans // TILE) for f in range(frames)]
        for count, (f, n) in enumerate(products):
            columns = slice(n * TILE, (n + 1) * TILE)
            taps = [t for t in range(3) if 0 <= f + t - 1 < frames]
            left = jnp.concatenate([lhs[(f + t - 1) * block : (f + t) * block, part] for t in taps], 1)
            right = jnp.concatenate([weight[t, part, columns] for t in taps], 0)
            v = jnp.dot(left, right, preferred_element_type=jnp.float32)
            if k:
                v = v + pre[f * block : (f + 1) * block, columns]
            pre[f * block : (f + 1) * block, columns] = v
            done, todo = len(pieces) * count // len(products), len(pieces) * (count + 1) // len(products)
            for piece in pieces[done:todo]:
                piece()
            if k + 1 == chunks:
                if late:
                    late.pop(0)()
                late.append(activate(f, columns))
                if f == 1 and n:
                    parts.append(project(slice((n - 1) * TILE, n * TILE))())
    late.pop(0)()
    parts.append(project(slice(chans - TILE, chans))())
    video = functools.reduce(lambda a, b: a + b, parts)
    vnorm = jnp.sqrt(jnp.sum(video * video, axis=1, keepdims=True) + 1e-06)
    vunit = video / vnorm
    unit[0:8, :] = vunit
    unit[8:16, :] = jnp.broadcast_to(vnorm, vunit.shape)
    joined[caps_dev : caps_dev + clip_dev, :] = vunit[0:clip_dev]
    pack[...] = joined[...].astype(jnp.bfloat16)


def slope_kernel(pre, slope):
    v = pre[...]
    square = v * v
    t = jnp.tanh(GELU_A * v * (1.0 + GELU_B * square))
    inner = GELU_A * (1.0 + 3.0 * GELU_B * square)
    slope[...] = (0.5 + 0.5 * t + 0.5 * v * (1.0 - t * t) * inner).astype(jnp.bfloat16)


def backward_kernel(
    dims, every, unit, own, slope, delta, weight, proj, out_hbm, loss,
    out, lhs, acc, natural, colsum, sems,
):
    clip_dev, frames, pix, chans, block, caps_dev = dims
    dense, tiles = clip_dev * pix, chans // LANES
    real = frames * pix
    group = caps_dev + clip_dev
    wide = every.shape[0]
    step = 16 * group
    colsum[...] = jnp.zeros_like(colsum)

    def part(b, carry):
        chunk = every[pl.ds(pl.multiple_of(b * step, step), step), :]
        s = lax.dot_general(chunk, every[...], (((1,), (1,)), ((), ())), preferred_element_type=jnp.float32)
        row = lax.broadcasted_iota(jnp.int32, (step, 1), 0) % group
        colsum[...] += jnp.sum(jnp.where(row >= caps_dev, jnp.exp(s * INV_TEMP), 0.0), axis=0, keepdims=True)
        return carry

    lax.fori_loop(0, wide // step, part, 0)
    mine = every[group - 8 : group, :]
    scores = lax.dot_general(mine, every[...], (((1,), (1,)), ((), ())), preferred_element_type=jnp.float32) * INV_TEMP
    column = lax.broadcasted_iota(jnp.int32, (1, wide), 1)
    line = lax.broadcasted_iota(jnp.int32, (8, 1), 0)
    expo = jnp.where(column % group < caps_dev, jnp.exp(scores), 0.0)
    owns = jnp.concatenate([own[...], jnp.zeros((8, wide - own.shape[1]), jnp.float32)], 1)
    sums = jnp.where(column % group < caps_dev, colsum[...], 1.0)
    total = jnp.sum(expo, axis=1, keepdims=True)
    owned = owns * expo
    positive = jnp.sum(owned, axis=1, keepdims=True)
    text = jnp.sum(owns * (jnp.log(sums) - scores), axis=1, keepdims=True)
    safe = jnp.where(line >= 8 - clip_dev, positive, 1.0)
    value = jnp.log(total) - jnp.log(safe) + 0.2 * text
    place = lax.broadcasted_iota(jnp.int32, (8, LANES), 1) + (8 - clip_dev)
    picked = jnp.sum(jnp.where(place == line, value, 0.0), axis=0, keepdims=True)
    loss[...] = picked[:, 0:clip_dev]
    coef = expo / total - owned / safe + 0.2 * (expo / sums - owns)
    grad = INV_TEMP * jnp.dot(coef.astype(jnp.bfloat16), every[...], preferred_element_type=jnp.float32)
    vunit = unit[0:8, :]
    vnorm = unit[8:16, :]
    grad_video = ((grad - vunit * jnp.sum(vunit * grad, axis=1, keepdims=True)) / vnorm).astype(jnp.bfloat16)
    grad_pooled = lax.dot_general(
        grad_video, proj[...], (((1,), (1,)), ((), ())), preferred_element_type=jnp.float32
    ) * (1.0 / real)
    clip = clip_of((block, 1), 0, pix, clip_dev)
    spread = jnp.zeros((block, chans), jnp.float32)
    for i in range(clip_dev):
        spread = jnp.where(clip == i, grad_pooled[8 - clip_dev + i : 9 - clip_dev + i, :], spread)
    for f in range(frames):
        rows = slice(f * block, (f + 1) * block)
        lhs[rows, :] = (slope[rows, :].astype(jnp.float32) * spread).astype(jnp.bfloat16)
    rest = (frames - 1) * block
    turned = (((1,), (1,)), ((), ()))
    acc[...] = lax.dot_general(lhs[...], weight[1], turned, preferred_element_type=jnp.float32)
    acc[0:rest, :] += lax.dot_general(lhs[block:, :], weight[0], turned, preferred_element_type=jnp.float32)
    acc[block:, :] += lax.dot_general(lhs[0:rest, :], weight[2], turned, preferred_element_type=jnp.float32)
    squares = jnp.zeros((block, chans), jnp.float32)
    for f in range(frames):
        v = acc[f * block : (f + 1) * block, :]
        squares = squares + v * v
    squares = jnp.sum(squares, axis=1, keepdims=True)
    scale = jnp.zeros((block, 1), jnp.float32)
    for i in range(clip_dev):
        mean = jnp.sum(jnp.where(clip == i, squares, 0.0), axis=0, keepdims=True) * (1.0 / (real * chans))
        scale = jnp.where(clip == i, lax.rsqrt(mean + 1e-06), scale)
    scale = jnp.broadcast_to(scale, (block, LANES))[0:dense]
    for j in range(tiles):
        lanes = slice(j * LANES, (j + 1) * LANES)
        for f in range(frames):
            natural[j, pl.ds(f, dense, stride=frames), :] = acc[f * block : f * block + dense, lanes] * scale
    copies = []
    for low in range(0, dense, 56):
        high = min(low + 56, dense)
        rows = slice(low * frames, high * frames)
        for j in range(tiles):
            value = (natural[j, rows, :] + delta[j, rows, :]).astype(jnp.bfloat16)
            out[low:high, :, j * LANES : (j + 1) * LANES] = value.reshape(high - low, frames, LANES)
        copies.append(pltpu.make_async_copy(out.at[low:high], out_hbm.at[low:high], sems.at[low // 56]))
        copies[-1].start()
    for copy in copies:
        copy.wait()


def swap(held, blocks, steps):
    parts = [lax.ppermute(held, "dp", [(i, i ^ step) for i in range(blocks)]) for step in steps]
    return jnp.concatenate([held] + parts, 0)


def shards(blocks, clips, sign_seeds, time_weight, proj_weight, captions, caption_rows):
    clip_dev, frames, pix, chans = clips.shape
    caps_dev, embed = captions.shape
    dense = clip_dev * pix
    block = -(-dense // 8) * 8
    total = frames * block
    group = caps_dev + clip_dev
    tiles = chans // LANES
    bf16, f32, i32 = jnp.bfloat16, jnp.float32, jnp.int32
    shape = jax.ShapeDtypeStruct
    vmem = pl.BlockSpec(memory_space=pltpu.VMEM)
    hbm = pl.BlockSpec(memory_space=pltpu.HBM)
    pack, unit, pre, delta, own, weight, proj = pl.pallas_call(
        functools.partial(forward_kernel, (clip_dev, frames, pix, chans, block)),
        out_shape=(
            shape((group, embed), bf16),
            shape((16, embed), f32),
            shape((total, chans), f32),
            shape((tiles, dense * frames, LANES), f32),
            shape((8, -(-caps_dev // LANES) * LANES), f32),
            shape((3, chans, chans), bf16),
            shape((chans, embed), bf16),
        ),
        in_specs=[hbm] * 6,
        out_specs=(vmem,) * 7,
        scratch_shapes=[
            pltpu.VMEM((dense * frames, LANES), i32),
            pltpu.SMEM((clip_dev,), i32),
            pltpu.SMEM(caption_rows.shape, i32),
            pltpu.VMEM((tiles, dense, frames, LANES), bf16),
            pltpu.VMEM((caps_dev, embed), bf16),
            pltpu.VMEM((tiles, dense * frames, LANES), f32),
            pltpu.VMEM((total, chans), bf16),
            pltpu.VMEM((block, chans), f32),
            pltpu.VMEM((group, embed), f32),
            pltpu.SemaphoreType.DMA((tiles,)),
            pltpu.SemaphoreType.DMA((chans // CHUNK,)),
            pltpu.SemaphoreType.DMA((4,)),
        ],
        compiler_params=pltpu.CompilerParams(vmem_limit_bytes=28 << 20),
        name="forward",
    )(*[
        pltpu.with_memory_space_constraint(operand, pltpu.HBM)
        for operand in (
            sign_seeds,
            caption_rows,
            clips.transpose(0, 2, 1, 3).reshape(dense, frames, chans),
            time_weight,
            proj_weight,
            captions,
        )
    ])
    slope = pl.pallas_call(
        slope_kernel,
        out_shape=shape((total, chans), bf16),
        in_specs=[vmem],
        out_specs=vmem,
        compiler_params=pltpu.CompilerParams(vmem_limit_bytes=8 << 20),
        cost_estimate=pl.CostEstimate(flops=16 * total * chans, bytes_accessed=6 * total * chans, transcendentals=total * chans),
        name="slope",
    )(pre)
    if blocks == 16:
        rounds = [(8,), (2, 4, 6), (1,)]
    else:
        rounds = [(1 << b,) for b in reversed(range(blocks.bit_length() - 1))]
    every = pack
    for i, steps in enumerate(rounds):
        every = swap(every, blocks, steps)
        if i == 0:
            every, slope = lax.optimization_barrier((every, slope))
    out, loss = pl.pallas_call(
        functools.partial(backward_kernel, (clip_dev, frames, pix, chans, block, caps_dev)),
        out_shape=(shape((dense, frames, chans), bf16), shape((1, clip_dev), f32)),
        in_specs=[vmem] * 7,
        out_specs=(hbm, vmem),
        scratch_shapes=[
            pltpu.VMEM((dense, frames, chans), bf16),
            pltpu.VMEM((total, chans), bf16),
            pltpu.VMEM((total, chans), f32),
            pltpu.VMEM((tiles, dense * frames, LANES), f32),
            pltpu.VMEM((1, blocks * group), f32),
            pltpu.SemaphoreType.DMA((-(-dense // 56),)),
        ],
        compiler_params=pltpu.CompilerParams(vmem_limit_bytes=24 << 20),
        name="backward",
    )(every, unit, own, slope, delta, weight, proj)
    out = out.reshape(clip_dev, pix, frames, chans).transpose(0, 2, 1, 3)
    return out, loss.reshape(clip_dev)


def solution(mesh):
    in_specs = (
        P(("groups", "dp"), None, None, None),
        P(("groups", "dp")),
        P(),
        P(),
        P(("groups", "dp"), None),
        P(("groups", "dp"), None),
    )
    out_specs = (P(("groups", "dp"), None, None, None), P(("groups", "dp")))
    return jax.shard_map(
        functools.partial(shards, mesh.shape["dp"]),
        mesh=mesh,
        in_specs=in_specs,
        out_specs=out_specs,
        check_vma=False,
    )
```

```python
import functools

import jax
import jax.numpy as jnp
from jax import lax
from jax.experimental import pallas as pl
from jax.experimental.pallas import tpu as pltpu
from jax.sharding import PartitionSpec as P

INV_TEMP = 1.0 / 0.07
GELU_A = 0.7978845608028654
GELU_B = 0.044715
LANES = 128
CHUNK = 512
TILE = 512
HASH_STEP = 374761393
HASH_SEED = -1640531535
HASH_MIX = 668265263


def wrap(value):
    return jnp.int32((value + 2**31) % 2**32 - 2**31)


def signs(mixed):
    mixed = mixed ^ (mixed >> 13)
    mixed = mixed * jnp.int32(HASH_MIX)
    mixed = mixed ^ (mixed >> 16)
    return jnp.where((mixed & 128) != 0, jnp.float32(0.1), jnp.float32(-0.1))


def clip_of(shape, dim, pix, clip_dev):
    return lax.broadcasted_iota(jnp.int32, shape, dim) // pix


def forward_kernel(
    dims, seeds_hbm, rows_hbm, clips_hbm, weight_hbm, proj_hbm, captions_hbm,
    pack, unit, pre, delta, own, weight, proj,
    start, seeds, rows, clips, captions, natural, lhs, active, joined, clip_sems, weight_sems, sems,
):
    clip_dev, frames, pix, chans, block = dims
    dense, tiles = clip_dev * pix, chans // LANES
    caps_dev = captions.shape[0]
    per_chunk = CHUNK // LANES
    small = [
        pltpu.make_async_copy(src, dst, sems.at[i])
        for i, (src, dst) in enumerate(
            [(seeds_hbm, seeds), (rows_hbm, rows), (captions_hbm, captions), (proj_hbm, proj)]
        )
    ]
    clip_copies = [
        pltpu.make_async_copy(clips_hbm.at[:, :, j * LANES : (j + 1) * LANES], clips.at[j], clip_sems.at[j])
        for j in range(tiles)
    ]
    weight_copies = [
        pltpu.make_async_copy(
            weight_hbm.at[:, k * CHUNK : (k + 1) * CHUNK, :],
            weight.at[:, k * CHUNK : (k + 1) * CHUNK, :],
            weight_sems.at[k],
        )
        for k in range(chans // CHUNK)
    ]
    chunks = chans // CHUNK

    def fetch(k):
        for copy in clip_copies[k * per_chunk : (k + 1) * per_chunk]:
            copy.start()
        weight_copies[k].start()

    small[0].start()
    fetch(0)
    for copy in small[1:3]:
        copy.start()
    fetch(1)
    small[3].start()
    for f in range(frames):
        lhs[f * block + dense : (f + 1) * block, :] = jnp.zeros((block - dense, chans), jnp.bfloat16)
    row = lax.broadcasted_iota(jnp.int32, (dense * frames, LANES), 0)
    spot = row // frames
    clip = spot // pix
    first = ((row % frames) * pix + spot - clip * pix) * chans + lax.broadcasted_iota(jnp.int32, row.shape, 1)
    small[0].wait()
    seed = jnp.zeros(row.shape, jnp.int32)
    for i in range(clip_dev):
        seed = jnp.where(clip == i, seeds[i], seed)
    start[...] = seed * jnp.int32(HASH_SEED) + first * jnp.int32(HASH_STEP)
    for j in range(tiles):
        delta[j] = signs(start[...] + wrap(j * LANES * HASH_STEP))

    def hash_piece(j, rows):
        def run():
            x = clips[j, rows.start // frames : rows.stop // frames].reshape(rows.stop - rows.start, LANES)
            natural[j, rows, :] = x.astype(jnp.float32) + delta[j, rows, :]

        return run

    def order_piece(j, f):
        def run():
            lhs[f * block : f * block + dense, j * LANES : (j + 1) * LANES] = natural[
                j, pl.ds(f, dense, stride=frames), :
            ].astype(jnp.bfloat16)

        return run

    def prepare(k):
        mine = range(k * per_chunk, (k + 1) * per_chunk)
        for j in mine:
            clip_copies[j].wait()
        length = dense * frames
        cut = next(c for c in (112, 56, 16, length) if length % c == 0)
        pieces = [hash_piece(j, slice(r, r + cut)) for j in mine for r in range(0, length, cut)]
        return pieces + [order_piece(j, f) for j in mine for f in range(frames)]

    def activate(f, columns):
        def run():
            v = pre[f * block : (f + 1) * block, columns]
            gelu = v * (0.5 + 0.5 * jnp.tanh(GELU_A * v * (1.0 + GELU_B * (v * v))))
            active[:, columns] = gelu if f == 0 else active[:, columns] + gelu

        return run

    def project(columns):
        def run():
            sums = []
            for i in range(clip_dev):
                low, high = i * pix // 8 * 8, min(-(-(i + 1) * pix // 8) * 8, block)
                row = lax.broadcasted_iota(jnp.int32, (high - low, 1), 0) + low
                inside = (row >= i * pix) & (row < (i + 1) * pix)
                sums.append(jnp.sum(jnp.where(inside, active[low:high, columns], 0.0), axis=0, keepdims=True))
            pooled = (jnp.concatenate(sums + sums, 0) * (1.0 / (frames * pix))).astype(jnp.bfloat16)
            return jnp.dot(pooled, proj[columns, :], preferred_element_type=jnp.float32)

        return run

    for piece in prepare(0):
        piece()
    small[1].wait()
    small[2].wait()
    places = [(i, c) for i in range(clip_dev) for c in range(rows.shape[1])]
    base = rows[0, 0]
    for i, c in places:
        base = jnp.minimum(base, rows[i, c])
    line = lax.broadcasted_iota(jnp.int32, own.shape, 0)
    column = lax.broadcasted_iota(jnp.int32, own.shape, 1) + base
    mine = jnp.zeros(own.shape, jnp.float32)
    for i, c in places:
        mine = jnp.where((line == 8 - clip_dev + i) & (column == rows[i, c]), 1.0, mine)
    own[...] = mine
    cap = captions[...].astype(jnp.float32)
    cap = cap / jnp.sqrt(jnp.sum(cap * cap, axis=1, keepdims=True) + 1e-06)
    joined[0:caps_dev, :] = cap
    late, parts = [], []
    for k in range(chunks):
        weight_copies[k].wait()
        if k + 2 < chunks:
            fetch(k + 2)
        pieces = prepare(k + 1) if k + 1 < chunks else []
        if k + 1 == chunks:
            small[3].wait()
        part = slice(k * CHUNK, (k + 1) * CHUNK)
        products = [(f, n) for n in range(chans // TILE) for f in range(frames)]
        for count, (f, n) in enumerate(products):
            columns = slice(n * TILE, (n + 1) * TILE)
            taps = [t for t in range(3) if 0 <= f + t - 1 < frames]
            left = jnp.concatenate([lhs[(f + t - 1) * block : (f + t) * block, part] for t in taps], 1)
            right = jnp.concatenate([weight[t, part, columns] for t in taps], 0)
            v = jnp.dot(left, right, preferred_element_type=jnp.float32)
            if k:
                v = v + pre[f * block : (f + 1) * block, columns]
            pre[f * block : (f + 1) * block, columns] = v
            done, todo = len(pieces) * count // len(products), len(pieces) * (count + 1) // len(products)
            for piece in pieces[done:todo]:
                piece()
            if k + 1 == chunks:
                if late:
                    late.pop(0)()
                late.append(activate(f, columns))
                if f == 1 and n:
                    parts.append(project(slice((n - 1) * TILE, n * TILE))())
    late.pop(0)()
    parts.append(project(slice(chans - TILE, chans))())
    video = functools.reduce(lambda a, b: a + b, parts)
    vnorm = jnp.sqrt(jnp.sum(video * video, axis=1, keepdims=True) + 1e-06)
    vunit = video / vnorm
    unit[0:8, :] = vunit
    unit[8:16, :] = jnp.broadcast_to(vnorm, vunit.shape)
    joined[caps_dev : caps_dev + clip_dev, :] = vunit[0:clip_dev]
    pack[...] = joined[...].astype(jnp.bfloat16)


def slope_kernel(pre, slope):
    v = pre[...]
    square = v * v
    t = jnp.tanh(GELU_A * v * (1.0 + GELU_B * square))
    inner = GELU_A * (1.0 + 3.0 * GELU_B * square)
    slope[...] = (0.5 + 0.5 * t + 0.5 * v * (1.0 - t * t) * inner).astype(jnp.bfloat16)


def backward_kernel(
    dims, every, unit, own, slope, delta, weight, proj, out_hbm, loss,
    out, lhs, acc, natural, colsum, sems,
):
    clip_dev, frames, pix, chans, block, caps_dev = dims
    dense, tiles = clip_dev * pix, chans // LANES
    real = frames * pix
    group = caps_dev + clip_dev
    wide = every.shape[0]
    step = 16 * group
    colsum[...] = jnp.zeros_like(colsum)

    def part(b, carry):
        chunk = every[pl.ds(pl.multiple_of(b * step, step), step), :]
        s = lax.dot_general(chunk, every[...], (((1,), (1,)), ((), ())), preferred_element_type=jnp.float32)
        row = lax.broadcasted_iota(jnp.int32, (step, 1), 0) % group
        colsum[...] += jnp.sum(jnp.where(row >= caps_dev, jnp.exp(s * INV_TEMP), 0.0), axis=0, keepdims=True)
        return carry

    lax.fori_loop(0, wide // step, part, 0)
    mine = every[group - 8 : group, :]
    scores = lax.dot_general(mine, every[...], (((1,), (1,)), ((), ())), preferred_element_type=jnp.float32) * INV_TEMP
    column = lax.broadcasted_iota(jnp.int32, (1, wide), 1)
    line = lax.broadcasted_iota(jnp.int32, (8, 1), 0)
    expo = jnp.where(column % group < caps_dev, jnp.exp(scores), 0.0)
    owns = jnp.concatenate([own[...], jnp.zeros((8, wide - own.shape[1]), jnp.float32)], 1)
    sums = jnp.where(column % group < caps_dev, colsum[...], 1.0)
    total = jnp.sum(expo, axis=1, keepdims=True)
    owned = owns * expo
    positive = jnp.sum(owned, axis=1, keepdims=True)
    text = jnp.sum(owns * (jnp.log(sums) - scores), axis=1, keepdims=True)
    safe = jnp.where(line >= 8 - clip_dev, positive, 1.0)
    value = jnp.log(total) - jnp.log(safe) + 0.2 * text
    place = lax.broadcasted_iota(jnp.int32, (8, LANES), 1) + (8 - clip_dev)
    picked = jnp.sum(jnp.where(place == line, value, 0.0), axis=0, keepdims=True)
    loss[...] = picked[:, 0:clip_dev]
    coef = expo / total - owned / safe + 0.2 * (expo / sums - owns)
    grad = INV_TEMP * jnp.dot(coef.astype(jnp.bfloat16), every[...], preferred_element_type=jnp.float32)
    vunit = unit[0:8, :]
    vnorm = unit[8:16, :]
    grad_video = ((grad - vunit * jnp.sum(vunit * grad, axis=1, keepdims=True)) / vnorm).astype(jnp.bfloat16)
    grad_pooled = lax.dot_general(
        grad_video, proj[...], (((1,), (1,)), ((), ())), preferred_element_type=jnp.float32
    ) * (1.0 / real)
    clip = clip_of((block, 1), 0, pix, clip_dev)
    spread = jnp.zeros((block, chans), jnp.float32)
    for i in range(clip_dev):
        spread = jnp.where(clip == i, grad_pooled[8 - clip_dev + i : 9 - clip_dev + i, :], spread)
    for f in range(frames):
        rows = slice(f * block, (f + 1) * block)
        lhs[rows, :] = (slope[rows, :].astype(jnp.float32) * spread).astype(jnp.bfloat16)
    rest = (frames - 1) * block
    turned = (((1,), (1,)), ((), ()))
    acc[...] = lax.dot_general(lhs[0 : rest + block, :], weight[1], turned, preferred_element_type=jnp.float32)
    acc[0:rest, :] += lax.dot_general(lhs[block : rest + block, :], weight[0], turned, preferred_element_type=jnp.float32)
    acc[block:, :] += lax.dot_general(lhs[0:rest, :], weight[2], turned, preferred_element_type=jnp.float32)
    squares = jnp.zeros((block, chans), jnp.float32)
    for f in range(frames):
        v = acc[f * block : (f + 1) * block, :]
        squares = squares + v * v
    squares = jnp.sum(squares, axis=1, keepdims=True)
    scale = jnp.zeros((block, 1), jnp.float32)
    for i in range(clip_dev):
        mean = jnp.sum(jnp.where(clip == i, squares, 0.0), axis=0, keepdims=True) * (1.0 / (real * chans))
        scale = jnp.where(clip == i, lax.rsqrt(mean + 1e-06), scale)
    scale = jnp.broadcast_to(scale, (block, LANES))[0:dense]
    for j in range(tiles):
        lanes = slice(j * LANES, (j + 1) * LANES)
        for f in range(frames):
            natural[j, pl.ds(f, dense, stride=frames), :] = acc[f * block : f * block + dense, lanes] * scale
    copies = []
    for low in range(0, dense, 56):
        high = min(low + 56, dense)
        rows = slice(low * frames, high * frames)
        for j in range(tiles):
            value = (natural[j, rows, :] + delta[j, rows, :]).astype(jnp.bfloat16)
            out[low:high, :, j * LANES : (j + 1) * LANES] = value.reshape(high - low, frames, LANES)
        copies.append(pltpu.make_async_copy(out.at[low:high], out_hbm.at[low:high], sems.at[low // 56]))
        copies[-1].start()
    for copy in copies:
        copy.wait()


def swap(held, blocks, steps):
    parts = [lax.ppermute(held, "dp", [(i, i ^ step) for i in range(blocks)]) for step in steps]
    return jnp.concatenate([held] + parts, 0)


def shards(blocks, clips, sign_seeds, time_weight, proj_weight, captions, caption_rows):
    clip_dev, frames, pix, chans = clips.shape
    caps_dev, embed = captions.shape
    dense = clip_dev * pix
    block = -(-dense // 8) * 8
    total = frames * block
    group = caps_dev + clip_dev
    tiles = chans // LANES
    bf16, f32, i32 = jnp.bfloat16, jnp.float32, jnp.int32
    shape = jax.ShapeDtypeStruct
    vmem = pl.BlockSpec(memory_space=pltpu.VMEM)
    hbm = pl.BlockSpec(memory_space=pltpu.HBM)
    pack, unit, pre, delta, own, weight, proj = pl.pallas_call(
        functools.partial(forward_kernel, (clip_dev, frames, pix, chans, block)),
        out_shape=(
            shape((group, embed), bf16),
            shape((16, embed), f32),
            shape((total, chans), f32),
            shape((tiles, dense * frames, LANES), f32),
            shape((8, -(-caps_dev // LANES) * LANES), f32),
            shape((3, chans, chans), bf16),
            shape((chans, embed), bf16),
        ),
        in_specs=[hbm] * 6,
        out_specs=(vmem,) * 7,
        scratch_shapes=[
            pltpu.VMEM((dense * frames, LANES), i32),
            pltpu.SMEM((clip_dev,), i32),
            pltpu.SMEM(caption_rows.shape, i32),
            pltpu.VMEM((tiles, dense, frames, LANES), bf16),
            pltpu.VMEM((caps_dev, embed), bf16),
            pltpu.VMEM((tiles, total, LANES), f32),
            pltpu.VMEM((total + 16, chans), bf16),
            pltpu.VMEM((block, chans), f32),
            pltpu.VMEM((group, embed), f32),
            pltpu.SemaphoreType.DMA((tiles,)),
            pltpu.SemaphoreType.DMA((chans // CHUNK,)),
            pltpu.SemaphoreType.DMA((4,)),
        ],
        compiler_params=pltpu.CompilerParams(vmem_limit_bytes=28 << 20),
        name="forward",
    )(*[
        pltpu.with_memory_space_constraint(operand, pltpu.HBM)
        for operand in (
            sign_seeds,
            caption_rows,
            clips.transpose(0, 2, 1, 3).reshape(dense, frames, chans),
            time_weight,
            proj_weight,
            captions,
        )
    ])
    slope = pl.pallas_call(
        slope_kernel,
        out_shape=shape((total, chans), bf16),
        in_specs=[vmem],
        out_specs=vmem,
        compiler_params=pltpu.CompilerParams(vmem_limit_bytes=8 << 20),
        cost_estimate=pl.CostEstimate(flops=16 * total * chans, bytes_accessed=6 * total * chans, transcendentals=total * chans),
        name="slope",
    )(pre)
    if blocks == 16:
        rounds = [(8,), (2, 4, 6), (1,)]
    else:
        rounds = [(1 << b,) for b in reversed(range(blocks.bit_length() - 1))]
    every = pack
    for i, steps in enumerate(rounds):
        every = swap(every, blocks, steps)
        if i == 0:
            every, slope = lax.optimization_barrier((every, slope))
    out, loss = pl.pallas_call(
        functools.partial(backward_kernel, (clip_dev, frames, pix, chans, block, caps_dev)),
        out_shape=(shape((dense, frames, chans), bf16), shape((1, clip_dev), f32)),
        in_specs=[vmem] * 7,
        out_specs=(hbm, vmem),
        scratch_shapes=[
            pltpu.VMEM((dense, frames, chans), bf16),
            pltpu.VMEM((total + 16, chans), bf16),
            pltpu.VMEM((total, chans), f32),
            pltpu.VMEM((tiles, total, LANES), f32),
            pltpu.VMEM((1, blocks * group), f32),
            pltpu.SemaphoreType.DMA((-(-dense // 56),)),
        ],
        compiler_params=pltpu.CompilerParams(vmem_limit_bytes=24 << 20),
        name="backward",
    )(every, unit, own, slope, delta, weight, proj)
    out = out.reshape(clip_dev, pix, frames, chans).transpose(0, 2, 1, 3)
    return out, loss.reshape(clip_dev)


def solution(mesh):
    in_specs = (
        P(("groups", "dp"), None, None, None),
        P(("groups", "dp")),
        P(),
        P(),
        P(("groups", "dp"), None),
        P(("groups", "dp"), None),
    )
    out_specs = (P(("groups", "dp"), None, None, None), P(("groups", "dp")))
    return jax.shard_map(
        functools.partial(shards, mesh.shape["dp"]),
        mesh=mesh,
        in_specs=in_specs,
        out_specs=out_specs,
        check_vma=False,
    )
```
